32 devices in a mesh: task: 16 (over z, x, core), tensor: 2 (over y).
Axes of the slice: x: 2, y: 2, z: 4, core: 2. Of those that a mesh axis runs over, the one named last changes fastest.
Arguments:
- inputs: bfloat16 [3072, 8192], P('task'), may hold values from -6 to 6
- queries: bfloat16 [3072, 4096], P('task', 'tensor'), may hold values from -6 to 6
- task_vectors: bfloat16 [8, 2, 8192, 1024], P(None, None, 'task', 'tensor'), may hold values from -0.0625 to 0.0625
- base_weights: bfloat16 [2, 8192, 1024], P(None, 'task', 'tensor'), may hold values from -0.0625 to 0.0625
- scale_exps: int32 [8, 2, 64, 8], P(None, None, 'task', 'tensor'), may hold values from -3 to 0
- coefs: float32 [8, 2], replicated, may hold values from 0.1 to 0.6
Outputs:
- attended: bfloat16 [3072, 4096], P('task', 'tensor')
- mean_entropy: float32 [], replicated
- coef_grad: float32 [8, 2], replicated
The draws below stay inside these ranges and needn't reach their ends.
All inputs are finite; a program needn't handle non-finite values.
Results may differ from the reference program's by a relative error of at most 0.0087.
Values may be sent and summed in bfloat16 or wider, within the bound.
A program may use at most 128 MiB of HBM per device.

```python
import math
import jax
import jax.numpy as jnp

D = 8192
HEAD = 128
KVH = 8
GROUP = 4
TASKS = 8
BLOCK = 128
TOK_DEV = 192
TOKENS = 3072
KVW = 1024
QW = 4096


def plant(result, stream_key, smallest, high):
    dims = result.shape
    index_at = [jax.random.randint(jax.random.fold_in(stream_key, axis), (), 0, dims[axis]) for axis in range(len(dims))]
    result = result.at[tuple(index_at)].set(smallest)
    longest = dims.index(max(dims))
    index_at[longest] = (index_at[longest] + 1) % dims[longest]
    return result.at[tuple(index_at)].set(high)


def block_levels(stream_key, shape, cuts, least, high):
    factor_of, own = 1.0, jax.random.fold_in(stream_key, 6)
    for axis_at, blocks in cuts:
        steps = jnp.exp(jax.random.uniform(jax.random.fold_in(own, axis_at), (blocks,), jnp.float32, least / len(cuts), high / len(cuts)))
        factor_of = factor_of * jnp.repeat(steps, shape[axis_at] // blocks).reshape([-1 if axis == axis_at else 1 for axis in range(len(shape))])
    return factor_of


def scatter_about(stream_key, extent, width, most, split=(), held_as=jnp.bfloat16):
    result = width * jax.random.normal(stream_key, extent, jnp.float32)
    if split:
        result = result * block_levels(stream_key, extent, split, -0.22, 0.18)
    return jnp.clip(result, -most, most).astype(held_as)


def setup_inputs(seed: int = 0) -> dict:
    key_list = jax.random.split(jax.random.key(seed), 7)
    inputs = scatter_about(key_list[0], (TOKENS, D), 1.0, 6.0, ((0, 16),))
    queries = scatter_about(key_list[1], (TOKENS, QW), 1.0, 6.0, ((0, 16), (1, 2)))
    task_vectors = scatter_about(key_list[2], (TASKS, 2, D, KVW), D ** -0.5, 0.0625, ((2, 16), (3, 2)))
    base_weights = scatter_about(key_list[3], (2, D, KVW), D ** -0.5, 0.0625, ((1, 16), (2, 2)))
    scale_exps = plant(jax.random.randint(key_list[4], (TASKS, 2, D // BLOCK, KVW // BLOCK), -3, 1), jax.random.fold_in(key_list[4], 1), -3, 0).astype(jnp.int32)
    coefs = jnp.clip(jnp.exp(jax.random.uniform(key_list[5], (TASKS, 2), jnp.float32, math.log(0.1), math.log(0.6))), 0.1, 0.6)
    return {"inputs": inputs, "queries": queries, "task_vectors": task_vectors, "base_weights": base_weights, "scale_exps": scale_exps, "coefs": coefs}


sharpen = 4.0
capping = 8.0
masked_value = -1e30


def dequantize(vectors, exponents):
    tasks, mats, rows, cols = vectors.shape
    row_blocks = exponents.shape[2]
    col_blocks = exponents.shape[3]
    factor = jnp.exp2(exponents.astype(jnp.float32))
    blocked = vectors.astype(jnp.float32).reshape(tasks, mats, row_blocks, rows // row_blocks, col_blocks, cols // col_blocks)
    blocked = blocked * factor[:, :, :, None, :, None]
    return blocked.reshape(tasks, mats, rows, cols)


def reference(inputs, queries, task_vectors, base_weights, scale_exps, coefs):
    scaled = dequantize(task_vectors, scale_exps)
    merged = (base_weights.astype(jnp.float32) + jnp.sum(coefs[:, :, None, None] * scaled, axis=0)).astype(jnp.bfloat16)
    keys_b = jnp.dot(inputs, merged[0], preferred_element_type=jnp.float32).astype(jnp.bfloat16)
    values_b = jnp.dot(inputs, merged[1], preferred_element_type=jnp.float32).astype(jnp.bfloat16)
    nseq = TOKENS // TOK_DEV
    query_all = queries.astype(jnp.float32).reshape(nseq, TOK_DEV, KVH, GROUP, HEAD)
    key_all = keys_b.astype(jnp.float32).reshape(nseq, TOK_DEV, KVH, HEAD)
    value_all = values_b.astype(jnp.float32).reshape(nseq, TOK_DEV, KVH, HEAD)
    inverse = HEAD ** -0.5
    scores = jnp.einsum('nshrd,nthd->nhrst', query_all, key_all) * inverse
    position = jnp.arange(TOK_DEV)
    causal = position[None, :] <= position[:, None]
    scores = jnp.where(causal, scores, masked_value)
    probs = jax.nn.softmax(scores, axis=-1)
    probs_b = probs.astype(jnp.bfloat16)
    outputs = jnp.einsum('nhrst,nthd->nshrd', probs_b.astype(jnp.float32), value_all)
    attended = outputs.astype(jnp.bfloat16).reshape(TOKENS, QW)
    logits = capping * jnp.tanh(sharpen * attended.astype(jnp.float32) / capping)
    expo = jnp.exp(logits)
    total = jnp.sum(expo, axis=1, keepdims=True)
    moment = jnp.sum(expo * logits, axis=1, keepdims=True)
    entropy = jnp.log(total[:, 0]) - moment[:, 0] / total[:, 0]
    mean_entropy = jnp.sum(entropy) / TOKENS
    slope = sharpen * (1.0 - (logits / capping) ** 2)
    d_out = (slope * (-(expo / total) * (logits - moment / total))).astype(jnp.bfloat16)
    d_out_f = d_out.astype(jnp.float32).reshape(nseq, TOK_DEV, KVH, GROUP, HEAD)
    d_probs = jnp.einsum('nshrd,nthd->nhrst', d_out_f, value_all)
    d_scores = (probs * (d_probs - jnp.sum(probs * d_probs, axis=-1, keepdims=True))).astype(jnp.bfloat16)
    d_keys = jnp.einsum('nhrst,nshrd->nthd', d_scores.astype(jnp.float32), query_all) * inverse
    d_values = jnp.einsum('nhrst,nshrd->nthd', probs_b.astype(jnp.float32), d_out_f)
    d_keys_b = d_keys.astype(jnp.bfloat16).reshape(TOKENS, KVW)
    d_values_b = d_values.astype(jnp.bfloat16).reshape(TOKENS, KVW)
    grad_keys = jnp.dot(inputs.T, d_keys_b, preferred_element_type=jnp.float32)
    grad_values = jnp.dot(inputs.T, d_values_b, preferred_element_type=jnp.float32)
    weight_grads = jnp.stack([grad_keys, grad_values])
    coef_grad = jnp.sum(weight_grads[None] * scaled, axis=(2, 3))
    return attended, mean_entropy, coef_grad
```

```python
import functools
import math

import jax
import jax.numpy as jnp
from jax import lax
from jax.experimental import pallas as pl
from jax.experimental.pallas import tpu as pltpu
from jax.sharding import PartitionSpec as P

HEAD = 128
GROUP = 4

sharpen = 4.0
capping = 8.0
masked_value = -1e30

MESH = pl.DeviceIdType.MESH
VMEM_BYTES = 60 * 1024 * 1024
F32 = jnp.float32
BF16 = jnp.bfloat16


def factors(n_task):
    outer = math.gcd(n_task, 4)
    mid = math.gcd(n_task // outer, 2)
    return outer, mid, n_task // (outer * mid)


def place(dims):
    _, mid, inner = dims
    task = lax.axis_index("task")
    rest = lax.rem(task, mid * inner)
    return task, task // (mid * inner), rest // inner, lax.rem(rest, inner)


def turned(value, step, size):
    return lax.rem(value + (step + size), size)


def flip(value, step):
    bit = 1
    for_value = value
    while bit <= step:
        if step & bit:
            for_value = for_value + bit - 2 * bit * lax.rem(value // bit, 2)
        bit *= 2
    return for_value


def scale_of(exps, t, m, i, j):
    return lax.shift_left(jnp.int32(1), exps[m, i, j, t] + 3).astype(F32) * 0.125


def chosen(table, value):
    total = 0
    for n, entry in enumerate(table):
        if not entry:
            continue
        term, bit = entry, 1
        while bit < len(table):
            digit = lax.rem(value // bit, 2)
            term = term * (digit if n & bit else 1 - digit)
            bit *= 2
        total = total + term
    return jnp.int32(total) if isinstance(total, int) else total


def line_order(outer):
    sources = [sorted((s for s in range(outer) if s != v), key=lambda s: abs(s - v)) for v in range(outer)]
    after = [[v + 1 if s < v else v - 1 for s in sources[v]] for v in range(outer)]
    steps = []
    for k in range(outer - 1):
        steps.append(
            (
                [sources[v][k] for v in range(outer)],
                [max(0, min(outer - 1, after[v][k])) for v in range(outer)],
                [int(0 <= after[v][k] < outer) for v in range(outer)],
            )
        )
    return steps


def index_of(dims, a, b, c):
    _, mid, inner = dims
    return (a * mid + b) * inner + c


def meet(peers):
    sem = pltpu.get_barrier_semaphore()
    for peer in peers:
        pl.semaphore_signal(sem, inc=1, device_id=peer, device_id_type=MESH)
    pl.semaphore_wait(sem, len(peers))


def send(src, dst, send_sem, recv_sem, peer):
    copy = pltpu.make_async_remote_copy(
        src_ref=src,
        dst_ref=dst,
        send_sem=send_sem,
        recv_sem=recv_sem,
        device_id=peer,
        device_id_type=MESH,
    )
    copy.start()
    return copy


def fetch(src, dst, sem):
    copy = pltpu.make_async_copy(src, dst, sem)
    copy.start()
    return copy


def project_stage(
    dims, n_tensor, pieces, bunch,
    inputs, vectors, base, exps, coefs, greet,
    kv_out, rows_out,
    xin, mg, vec_v, base_v, acc, hold, pout, pin,
    local_sem, keep_sem, x_send, x_recv, y_send, y_recv, g_send, g_recv, r_send, r_recv, p_send, p_recv,
):
    outer, mid, inner = dims
    group = mid * inner
    task, a, b, c = place(dims)
    y = lax.axis_index("tensor")
    mine = b * inner + c
    tasks, mats, rows, cols = vectors.shape
    row_blocks, col_blocks = exps.shape[1:3]
    tokens = inputs.shape[0]
    piece = tokens // pieces
    span = group * rows
    part = span // n_tensor
    turns = list(range(outer - 1, 0, -1))

    def at(a_, b_, c_):
        return {"task": index_of(dims, a_, b_, c_), "tensor": y}

    def tensor_peer(step):
        return {"task": task, "tensor": turned(y, step, n_tensor)}

    def group_peer(f, e):
        return at(a, turned(b, f, mid), turned(c, e, inner))

    def some(k):
        return slice(k * piece, (k + 1) * piece)

    def bunch_of(k):
        return slice(k * piece * bunch, (k + 1) * piece * bunch)

    base_copy = fetch(base, base_v, local_sem.at[0])
    vec_copies = [
        fetch(vectors.at[:, m], vec_v.at[:, m], local_sem.at[2 + m]) for m in range(mats)
    ]
    own_copy = fetch(
        inputs.at[:, pl.ds(pl.multiple_of(a * span, 128), span)], xin.at[a], local_sem.at[1]
    )
    greet()
    sent = []
    x_copies = {}
    own_cols = pl.ds(pl.multiple_of(y * part, 128), part)
    for k in range(pieces):
        for d in turns:
            to = flip(a, d)
            slot = d * pieces + k
            x_copies[k, d] = send(
                inputs.at[some(k), pl.ds(pl.multiple_of(to * span + y * part, 128), part)],
                xin.at[a, some(k), own_cols],
                x_send.at[slot], x_recv.at[slot], at(to, b, c),
            )
            sent.append(x_copies[k, d])
    high = rows // row_blocks
    wide = cols // col_blocks
    base_copy.wait()
    g_copies = {}

    def share(m, f, e, hop):
        came = turned(b, -(f - hop[0]), mid) * inner + turned(c, -(e - hop[1]), inner)
        slot = (m * mid + f) * inner + e
        g_copies[m, f, e] = send(
            mg.at[came, m], mg.at[came, m], g_send.at[slot], g_recv.at[slot], group_peer(*hop)
        )
        sent.append(g_copies[m, f, e])

    for m in range(mats):
        vec_copies[m].wait()

        def merge(i, carry):
            these = pl.ds(pl.multiple_of(i * high, 8), high)
            for j in range(col_blocks):
                across = slice(j * wide, (j + 1) * wide)
                total = base_v[m, these, across].astype(F32)
                for t in range(tasks):
                    scale = coefs[m, t] * scale_of(exps, t, m, i, j)
                    total += scale * vec_v[t, m, these, across].astype(F32)
                mg[mine, m, these, across] = total.astype(BF16)
            return carry

        lax.fori_loop(0, row_blocks, merge, 0)
        for f in range(1, mid):
            share(m, f, 0, (f, 0))
        for e in range(1, inner):
            share(m, 0, e, (0, e))

    r_copies = []
    keeps = []

    def spread(k, d):
        a_from = flip(a, d)
        owner = a_from * group + mine
        for f in range(mid):
            for e in range(inner):
                if not (f or e):
                    continue
                to = turned(b, f, mid) * inner + turned(c, e, inner)
                slot = ((k * outer + d) * mid + f) * inner + e
                r_copies.append(
                    send(
                        xin.at[a_from, bunch_of(k), pl.ds(pl.multiple_of(to * rows, 128), rows)],
                        rows_out.at[owner, bunch_of(k)],
                        r_send.at[slot], r_recv.at[slot], group_peer(f, e),
                    )
                )
        keeps.append(
            fetch(
                xin.at[a_from, bunch_of(k), pl.ds(pl.multiple_of(mine * rows, 128), rows)],
                rows_out.at[owner, bunch_of(k)],
                keep_sem.at[k * outer + d],
            )
        )

    y_copies = {}

    def pass_on(k):
        for d in turns:
            x_copies[k, d].wait_recv()
            block = xin.at[flip(a, d), some(k), own_cols]
            for s in range(1, n_tensor):
                slot = (k * outer + d) * n_tensor + s
                y_copies[k, d, s] = send(
                    block, block, y_send.at[slot], y_recv.at[slot], tensor_peer(s)
                )
                sent.append(y_copies[k, d, s])

    def share_on(m):
        for f in range(1, mid):
            g_copies[m, f, 0].wait_recv()
            for e in range(1, inner):
                share(m, f, e, (0, e))

    def own_part(m):
        for f in range(mid):
            for e in range(1, inner):
                g_copies[m, f, e].wait_recv()
        total = None
        for g in range(group):
            term = jnp.dot(
                xin[a, :, g * rows:(g + 1) * rows], mg[g, m], preferred_element_type=F32
            )
            total = term if total is None else total + term
        acc[m] = total

    p_copies = {}

    def give(k, m, d, to):
        slot = (d * pieces + k) * mats + m
        p_copies[k, m, d] = send(
            pout.at[d, m, some(k)], pin.at[d, m, some(k)],
            p_send.at[slot], p_recv.at[slot], at(flip(a, to), b, c),
        )
        sent.append(p_copies[k, m, d])

    def parts(k, m):
        if m == 0:
            for d in turns:
                for s in range(1, n_tensor):
                    y_copies[k, d, s].wait_recv()
        if not turns:
            return
        total = None
        for g in range(group):
            left = jnp.concatenate(
                [xin[flip(a, d), some(k), g * rows:(g + 1) * rows] for d in turns], axis=0
            )
            term = jnp.dot(left, mg[g, m], preferred_element_type=F32)
            total = term if total is None else total + term
        for n, d in enumerate(turns):
            mine_part = total[n * piece:(n + 1) * piece]
            if d == 2:
                hold[m, some(k)] = mine_part
            else:
                pout[d, m, some(k)] = mine_part.astype(BF16)
                give(k, m, d, 1)

    def combine(k, m):
        if 2 not in turns:
            return
        p_copies[k, m, 3].wait_recv()
        pout[2, m, some(k)] = (hold[m, some(k)] + pin[3, m, some(k)].astype(F32)).astype(BF16)
        give(k, m, 2, 2)

    last = pieces - 1

    def finish(m):
        for k in range(pieces):
            total = acc[m, some(k)]
            for d in turns:
                if d < 3:
                    p_copies[k, m, d].wait_recv()
                    total = total + pin[d, m, some(k)].astype(F32)
            kv_out[m, some(k)] = total.astype(BF16)

    done = {m: 0 for m in range(mats)}
    mixed = {m: 0 for m in range(mats)}
    spread_done = [0]

    def parts_to(m, count):
        while done[m] < min(count, pieces):
            parts(done[m], m)
            done[m] += 1
            while m == 0 and (spread_done[0] + 1) * bunch <= done[0]:
                for d in turns:
                    spread(spread_done[0], d)
                spread_done[0] += 1

    def combine_to(m, count):
        while mixed[m] < min(count, pieces):
            combine(mixed[m], m)
            mixed[m] += 1

    pass_on(0)
    own_copy.wait()
    for k in range(pieces // bunch):
        spread(k, 0)
    for k in range(1, pieces):
        if k == 2:
            share_on(0)
        pass_on(k)
        if k == 2:
            own_part(0)
        if k >= 2:
            parts_to(0, k)
        if k == 3:
            share_on(1)
            own_part(1)
        if k >= 4:
            parts_to(1, 2 * (k - 3))
        if k == 5:
            combine_to(0, 3)
    if pieces <= 2:
        share_on(0)
        own_part(0)
    parts_to(0, pieces)
    if pieces <= 3:
        share_on(1)
        own_part(1)
    combine_to(0, 4)
    parts_to(1, pieces)
    combine_to(0, pieces)

    def keys_ready():
        combine_to(1, pieces // 2)
        finish(0)

    def between(h, heads):
        combine_to(1, pieces // 2 + -(-(h + 1) * (pieces - pieces // 2) // heads))

    def values_ready():
        combine_to(1, pieces)
        finish(1)

    return sent, r_copies, keeps, keys_ready, between, values_ready


def attend_stage(
    n_tensor, queries, kv, att_out, dkv_out, probs, logs, expos, outs, sums, s_send, s_recv,
    keys_ready, between, values_ready, att_done, dkv_done,
):
    task = lax.axis_index("task")
    y = lax.axis_index("tensor")
    tokens = queries.shape[0]
    heads = kv.shape[2] // HEAD
    inverse = HEAD ** (-0.5)
    peers = [{"task": task, "tensor": turned(y, s, n_tensor)} for s in range(1, n_tensor)]
    key_at = lax.broadcasted_iota(jnp.int32, (tokens, GROUP * tokens), 0)
    query_at = lax.rem(lax.broadcasted_iota(jnp.int32, (tokens, GROUP * tokens), 1), tokens)
    causal = key_at <= query_at

    def stacked(h):
        return jnp.concatenate(
            [queries[:, (h * GROUP + r) * HEAD:(h * GROUP + r + 1) * HEAD] for r in range(GROUP)],
            axis=0,
        )

    keys_ready()
    for h in range(heads):
        cut = slice(h * HEAD, (h + 1) * HEAD)
        scores = lax.dot_general(
            kv[0, :, cut], stacked(h), (((1,), (1,)), ((), ())), preferred_element_type=F32
        ) * inverse
        scores = jnp.where(causal, scores, masked_value)
        weight = jnp.exp(scores - jnp.max(scores, axis=0, keepdims=True))
        probs[h] = weight * (1.0 / jnp.sum(weight, axis=0, keepdims=True))
        between(h, heads)
    values_ready()
    total = jnp.zeros((tokens, HEAD), F32)
    moment = jnp.zeros((tokens, HEAD), F32)
    for h in range(heads):
        cut = slice(h * HEAD, (h + 1) * HEAD)
        att = lax.dot_general(
            probs[h].astype(BF16), kv[1, :, cut], (((0,), (0,)), ((), ())), preferred_element_type=F32
        ).astype(BF16)
        logits = capping * jnp.tanh(sharpen * att.astype(F32) / capping)
        expo = jnp.exp(logits)
        logs[h] = logits
        expos[h] = expo
        scaled = expo * logits
        for r in range(GROUP):
            here = slice(r * tokens, (r + 1) * tokens)
            att_out[:, (h * GROUP + r) * HEAD:(h * GROUP + r + 1) * HEAD] = att[here]
            total += expo[here]
            moment += scaled[here]
    sums[y] = jnp.concatenate(
        [
            jnp.sum(total.T, axis=0, keepdims=True),
            jnp.sum(moment.T, axis=0, keepdims=True),
            jnp.zeros((6, tokens), F32),
        ],
        axis=0,
    )
    copies = [
        send(sums.at[y], sums.at[y], s_send.at[s], s_recv.at[s], peer)
        for s, peer in enumerate(peers)
    ]
    att_done()
    for copy in copies:
        copy.wait_recv()
    whole = sums[0]
    for s in range(1, n_tensor):
        whole = whole + sums[s]
    over = 1.0 / whole[0:1]
    average = whole[1:2] * over
    entropy = jnp.sum(jnp.log(whole[0:1]) - average)
    over_col = jnp.broadcast_to(over, (HEAD, tokens)).T
    average_col = jnp.broadcast_to(average, (HEAD, tokens)).T
    over_all = jnp.concatenate([over_col] * GROUP, axis=0)
    average_all = jnp.concatenate([average_col] * GROUP, axis=0)
    for h in range(heads):
        cut = slice(h * HEAD, (h + 1) * HEAD)
        logits = logs[h]
        slope = sharpen * (1.0 - (logits / capping) ** 2)
        d_out = (slope * (-(expos[h] * over_all) * (logits - average_all))).astype(BF16)
        outs[h] = d_out
        d_values = jnp.dot(probs[h].astype(BF16), d_out, preferred_element_type=F32)
        dkv_out[1, :, cut] = d_values.astype(BF16)
    dkv_done(1)
    for h in range(heads):
        cut = slice(h * HEAD, (h + 1) * HEAD)
        prob = probs[h]
        d_probs = lax.dot_general(
            kv[1, :, cut], outs[h], (((1,), (1,)), ((), ())), preferred_element_type=F32
        )
        d_scores = (
            prob * (d_probs - jnp.sum(prob * d_probs, axis=0, keepdims=True))
        ).astype(BF16)
        d_keys = jnp.dot(d_scores, stacked(h), preferred_element_type=F32) * inverse
        dkv_out[0, :, cut] = d_keys.astype(BF16)
    dkv_done(0)
    return copies, entropy


def spread_plan(dims, mats, dkv, got, g_send, g_recv, z_send, z_recv):
    outer, mid, inner = dims
    task, a, b, c = place(dims)
    y = lax.axis_index("tensor")
    steps = line_order(outer)
    planes = [a] + [chosen(source, a) for source, _, _ in steps]
    group = mid * inner
    started = []
    guarded = []

    def spot(plane, f, e):
        return index_of(dims, plane, turned(b, f, mid), turned(c, e, inner))

    def device(plane, f, e):
        return {"task": spot(plane, f, e), "tensor": y}

    def along(m, plane, target, slot):
        source = dkv.at[m] if plane is a else got.at[m, spot(plane, 0, 0)]
        return pltpu.make_async_remote_copy(
            src_ref=source,
            dst_ref=got.at[m, spot(plane, 0, 0)],
            send_sem=z_send.at[m * (outer + 1) + slot],
            recv_sem=z_recv.at[m * outer + plane],
            device_id=device(target, 0, 0),
            device_id_type=MESH,
        )

    def guard(copy, valid):
        @pl.when(valid == 1)
        def _():
            copy.start()

        guarded.append((copy, valid))

    copies = {}

    def forward(m, k, held_at, hop):
        where = index_of(
            dims, planes[k], turned(b, -held_at[0], mid), turned(c, -held_at[1], inner)
        )
        slot = (k, held_at[0] + hop[0], held_at[1] + hop[1])
        flat = ((m * outer + k) * mid + slot[1]) * inner + slot[2]
        own = k == 0 and held_at == (0, 0)
        copies[m, slot] = send(
            dkv.at[m] if own else got.at[m, where],
            got.at[m, where],
            g_send.at[flat], g_recv.at[flat], device(a, *hop),
        )
        started.append(copies[m, slot])

    def sent_own(m):
        for k in range(1, 2):
            if outer > 1:
                for step, slot in ((1, outer - 1), (-1, outer)):
                    valid = [int(0 <= v + step < outer) for v in range(outer)]
                    target = [max(0, min(outer - 1, v + step)) for v in range(outer)]
                    guard(along(m, a, chosen(target, a), slot), chosen(valid, a))
        for f in range(1, mid):
            forward(m, 0, (0, 0), (f, 0))
        for e in range(1, inner):
            forward(m, 0, (0, 0), (0, e))

    def arrive(m, k):
        plane = planes[k]
        _, target, valid = steps[k - 1]
        copy = along(m, plane, chosen(target, a), k - 1)
        copy.wait_recv()
        guard(copy, chosen(valid, a))
        for f in range(1, mid):
            forward(m, k, (0, 0), (f, 0))
        for e in range(1, inner):
            forward(m, k, (0, 0), (0, e))

    def across(m, k, f):
        copies[m, (k, f, 0)].wait_recv()
        for e in range(1, inner):
            forward(m, k, (f, 0), (0, e))

    def core(m, k, f, e):
        copies[m, (k, f, e)].wait_recv()

    def source(k, f, e):
        return index_of(dims, planes[k], turned(b, -f, mid), turned(c, -e, inner))

    def drain():
        for copy in started:
            copy.wait_send()
        for copy, valid in guarded:
            @pl.when(valid == 1)
            def _():
                copy.wait_send()

    return sent_own, arrive, across, core, source, drain


def reduce_stage(
    dims, n_tensor, task_peers, tensor_peers, rows_ready, entropy, plan,
    dkv, exps, grad_out, mean_out,
    got, rows_v, vec_v, grads, held, held_t,
    t_send, t_recv, y_send, y_recv,
):
    outer, mid, inner = dims
    n_task = outer * mid * inner
    task, a, b, c = place(dims)
    y = lax.axis_index("tensor")
    tasks, mats, rows, cols = vec_v.shape
    row_blocks, col_blocks = exps.shape[1:3]
    _, arrive, across, core, source, drain = plan
    fresh = set()

    def take(m, k, f, e):
        own = not (k or f or e)
        if k and not (f or e):
            arrive(m, k)
        elif f and not e:
            across(m, k, f)
        elif e:
            core(m, k, f, e)
        where = source(k, f, e)
        block = dkv[m] if own else got[m, where]
        term = lax.dot_general(
            rows_v[where], block, (((0,), (0,)), ((), ())), preferred_element_type=F32
        )
        if m in fresh:
            grads[m] += term
        else:
            grads[m] = term
            fresh.add(m)

    high = rows // row_blocks
    wide = cols // col_blocks

    def contracted(m):
        def contract(i, carry):
            these = pl.ds(pl.multiple_of(i * high, 8), high)
            carry = list(carry)
            for j in range(col_blocks):
                across = slice(j * wide, (j + 1) * wide)
                grad = grads[m, these, across]
                for t in range(tasks):
                    term = grad * vec_v[t, m, these, across].astype(F32)
                    term = jnp.sum(term.reshape(high // 8, 8, wide), axis=0)
                    carry[t] = carry[t] + scale_of(exps, t, m, i, j) * term
            return tuple(carry)

        start = tuple(jnp.zeros((8, wide), F32) for _ in range(tasks))
        return lax.fori_loop(0, row_blocks, contract, start)

    rows_ready()
    lines = {}
    turns = [(k, m) for k in range(outer) for m in reversed(range(mats))]
    for step in range(len(turns) + 2):
        slots = []
        if step < len(turns):
            slots.append((turns[step], 0, 0))
        if 1 <= step <= len(turns):
            slots += [(turns[step - 1], f, 0) for f in range(1, mid)]
            slots += [(turns[step - 1], 0, e) for e in range(1, inner)]
        if step >= 2:
            slots += [(turns[step - 2], f, e) for f in range(1, mid) for e in range(1, inner)]
        for (k, m), f, e in slots:
            take(m, k, f, e)
        if step - 2 >= len(turns) - mats:
            m = turns[step - 2][1]
            lines[m] = contracted(m)
    parts = [
        jnp.sum(lines[m][t], axis=0, keepdims=True) for t in range(tasks) for m in range(mats)
    ]
    entropy = jnp.broadcast_to(entropy / (n_tensor * wide), (1, wide))
    pad = -(len(parts) + 1) % 8
    stack = jnp.concatenate(parts + [entropy, jnp.zeros((pad, wide), F32)], axis=0)
    column = jnp.sum(stack, axis=1, keepdims=True)
    shape = (stack.shape[0], held.shape[2])
    along = lax.broadcasted_iota(jnp.int32, shape, 0) == lax.broadcasted_iota(jnp.int32, shape, 1)
    line = jnp.sum(jnp.where(along, column, 0.0), axis=0, keepdims=True)
    held[task] = jnp.broadcast_to(line, held.shape[1:])
    last = [
        send(held.at[task], held.at[task], t_send.at[s], t_recv.at[s], peer)
        for s, peer in enumerate(task_peers)
    ]
    for copy in last:
        copy.wait_recv()
    total = held[0]
    for k in range(1, n_task):
        total = total + held[k]
    held_t[y] = total
    more = [
        send(held_t.at[y], held_t.at[y], y_send.at[s], y_recv.at[s], peer)
        for s, peer in enumerate(tensor_peers)
    ]
    for copy in more:
        copy.wait_recv()
    total = held_t[0]
    for k in range(1, n_tensor):
        total = total + held_t[k]
    tokens = rows_v.shape[1]
    mean_out[...] = total[0:1, tasks * mats:tasks * mats + 1] * (1.0 / (tokens * n_task))
    wide_line = jnp.broadcast_to(total[0:1], (tasks, total.shape[1]))
    spot = lax.broadcasted_iota(jnp.int32, wide_line.shape, 1)
    task_at = lax.broadcasted_iota(jnp.int32, wide_line.shape, 0)
    grid = (mats, total.shape[1])
    mat_at = lax.broadcasted_iota(jnp.int32, grid, 0)
    result = jnp.zeros(grid, F32)
    for m in range(mats):
        column = jnp.sum(jnp.where(spot == mats * task_at + m, wide_line, 0.0), axis=1, keepdims=True)
        row = jnp.sum(jnp.where(spot == task_at, column, 0.0), axis=0, keepdims=True)
        result = jnp.where(mat_at == m, row, result)
    grad_out[...] = result[:, :tasks]
    drain()
    return last + more


def whole_kernel(
    dims, n_tensor, pieces, bunch,
    inputs, queries, vectors, base, exps, coefs,
    att, mean_out, grad_out,
    xin, mg, vec_v, base_v, acc, hold, pout, pin, kv, rows_v, dkv, probs, logs, expos, outs, sums,
    got, grads, held, held_t, q_v, att_v, io_sem, smem_sem, exps_v, coefs_v,
    local_sem, keep_sem, x_send, x_recv, y_send, y_recv, g_send, g_recv, r_send, r_recv, p_send, p_recv,
    s_send, s_recv, d_send, d_recv, l_send, l_recv, t_send, t_recv, z_send, z_recv,
):
    n_task = dims[0] * dims[1] * dims[2]
    task = lax.axis_index("task")
    y = lax.axis_index("tensor")
    task_peers = [{"task": turned(task, s, n_task), "tensor": y} for s in range(1, n_task)]
    tensor_peers = [{"task": task, "tensor": turned(y, s, n_tensor)} for s in range(1, n_tensor)]

    small = [fetch(exps, exps_v, smem_sem.at[0]), fetch(coefs, coefs_v, smem_sem.at[1])]
    waiting = []

    def greet():
        meet(task_peers + tensor_peers)
        for copy in small:
            copy.wait()

    query_copy = fetch(queries, q_v, io_sem.at[0])
    sent, r_copies, keeps, keys_ready, between, values_ready = project_stage(
        dims, n_tensor, pieces, bunch, inputs, vectors, base, exps_v, coefs_v, greet, kv, rows_v,
        xin, mg, vec_v, base_v, acc, hold, pout, pin,
        local_sem, keep_sem, x_send, x_recv, y_send, y_recv, g_send, g_recv, r_send, r_recv, p_send, p_recv,
    )
    query_copy.wait()
    plan = spread_plan(dims, kv.shape[0], dkv, got, d_send, d_recv, l_send, l_recv)

    def att_done():
        waiting.append(fetch(att_v, att, io_sem.at[1]))

    exchanged, entropy = attend_stage(
        n_tensor, q_v, kv, att_v, dkv, probs, logs, expos, outs, sums, s_send, s_recv,
        keys_ready, between, values_ready, att_done, plan[0],
    )

    def rows_ready():
        for copy in keeps:
            copy.wait()
        for copy in r_copies:
            copy.wait_recv()

    more = reduce_stage(
        dims, n_tensor, task_peers, tensor_peers, rows_ready, entropy, plan,
        dkv, exps_v, grad_out, mean_out,
        got, rows_v, vec_v, grads, held, held_t,
        t_send, t_recv, z_send, z_recv,
    )
    for copy in sent + r_copies + exchanged + more:
        copy.wait_send()
    for copy in waiting:
        copy.wait()


def local(inputs, queries, task_vectors, base_weights, scale_exps, coefs):
    n_task = lax.axis_size("task")
    n_tensor = lax.axis_size("tensor")
    dims = factors(n_task)
    outer, mid, inner = dims
    group = mid * inner
    tokens = inputs.shape[0]
    tasks, mats, rows, cols = task_vectors.shape
    heads = cols // HEAD
    pieces = math.gcd(tokens // 16, 6)
    bunch = math.gcd(pieces, 2)
    hbm = pl.BlockSpec(memory_space=pl.ANY)
    vmem = pl.BlockSpec(memory_space=pltpu.VMEM)
    dma = pltpu.SemaphoreType.DMA

    def pair(count):
        return [dma((count,)), dma((count,))]

    attended, mean_entropy, coef_grad = pl.pallas_call(
        functools.partial(whole_kernel, dims, n_tensor, pieces, bunch),
        out_shape=(
            jax.ShapeDtypeStruct(queries.shape, BF16),
            jax.ShapeDtypeStruct((1, 1), F32),
            jax.ShapeDtypeStruct((mats, tasks), F32),
        ),
        in_specs=[hbm] * 6,
        out_specs=(hbm, vmem, vmem),
        scratch_shapes=[
            pltpu.VMEM((outer, tokens, group * rows), BF16),
            pltpu.VMEM((group, mats, rows, cols), BF16),
            pltpu.VMEM(task_vectors.shape, BF16),
            pltpu.VMEM(base_weights.shape, BF16),
            pltpu.VMEM((mats, tokens, cols), F32),
            pltpu.VMEM((mats, tokens, cols), F32),
            pltpu.VMEM((outer, mats, tokens, cols), BF16),
            pltpu.VMEM((outer, mats, tokens, cols), BF16),
            pltpu.VMEM((mats, tokens, cols), BF16),
            pltpu.VMEM((n_task, tokens, rows), BF16),
            pltpu.VMEM((mats, tokens, cols), BF16),
            pltpu.VMEM((heads, tokens, GROUP * tokens), F32),
            pltpu.VMEM((heads, GROUP * tokens, HEAD), F32),
            pltpu.VMEM((heads, GROUP * tokens, HEAD), F32),
            pltpu.VMEM((heads, GROUP * tokens, HEAD), BF16),
            pltpu.VMEM((n_tensor, 8, tokens), F32),
            pltpu.VMEM((mats, n_task, tokens, cols), BF16),
            pltpu.VMEM((mats, rows, cols), F32),
            pltpu.VMEM((n_task, 8, 128), F32),
            pltpu.VMEM((n_tensor, 8, 128), F32),
            pltpu.VMEM(queries.shape, BF16),
            pltpu.VMEM(queries.shape, BF16),
            dma((2,)),
            dma((2,)),
            pltpu.SMEM((mats, *scale_exps.shape[2:], tasks), jnp.int32), pltpu.SMEM((mats, tasks), F32),
            dma((2 + mats,)), dma((pieces * outer,)),
            *pair(outer * pieces),
            *pair(pieces * outer * n_tensor),
            *pair(mats * group),
            *pair((pieces // bunch) * n_task),
            *pair(outer * pieces * mats),
            *pair(n_tensor),
            *pair(mats * n_task),
            dma((mats * (outer + 1),)), dma((mats * outer,)),
            *pair(n_task),
            *pair(n_tensor),
        ],
        compiler_params=pltpu.CompilerParams(
            collective_id=0, has_side_effects=True, vmem_limit_bytes=VMEM_BYTES
        ),
        name="whole",
    )(inputs, queries, task_vectors, base_weights, scale_exps.transpose(1, 2, 3, 0), coefs.T)
    return (attended, mean_entropy[0, 0], coef_grad.T)


def solution(mesh):
    return jax.shard_map(
        local,
        mesh=mesh,
        in_specs=(
            P("task", None),
            P("task", "tensor"),
            P(None, None, "task", "tensor"),
            P(None, "task", "tensor"),
            P(None, None, "task", "tensor"),
            P(),
        ),
        out_specs=(P("task", "tensor"), P(), P()),
        check_vma=False,
    )
```

```python
import functools
import math

import jax
import jax.numpy as jnp
from jax import lax
from jax.experimental import pallas as pl
from jax.experimental.pallas import tpu as pltpu
from jax.sharding import PartitionSpec as P

HEAD = 128
GROUP = 4

sharpen = 4.0
capping = 8.0
masked_value = -1e30

MESH = pl.DeviceIdType.MESH
VMEM_BYTES = 48 * 1024 * 1024
F32 = jnp.float32
BF16 = jnp.bfloat16


def factors(n_task):
    outer = math.gcd(n_task, 4)
    mid = math.gcd(n_task // outer, 2)
    return outer, mid, n_task // (outer * mid)


def place(dims):
    _, mid, inner = dims
    task = lax.axis_index("task")
    rest = lax.rem(task, mid * inner)
    return task, task // (mid * inner), rest // inner, lax.rem(rest, inner)


def turned(value, step, size):
    return lax.rem(value + (step + size), size)


def flip(value, step):
    bit = 1
    for_value = value
    while bit <= step:
        if step & bit:
            for_value = for_value + bit - 2 * bit * lax.rem(value // bit, 2)
        bit *= 2
    return for_value


def scale_of(exps, t, m, i, j):
    return lax.shift_left(jnp.int32(1), exps[m, i, j, t] + 3).astype(F32) * 0.125


def chosen(table, value):
    total = 0
    for n, entry in enumerate(table):
        if not entry:
            continue
        term, bit = entry, 1
        while bit < len(table):
            digit = lax.rem(value // bit, 2)
            term = term * (digit if n & bit else 1 - digit)
            bit *= 2
        total = total + term
    return jnp.int32(total) if isinstance(total, int) else total


def line_order(outer):
    sources = [sorted((s for s in range(outer) if s != v), key=lambda s: (abs(s - v), s if 2 * v < outer else -s)) for v in range(outer)]
    after = [[v + 1 if s < v else v - 1 for s in sources[v]] for v in range(outer)]
    steps = []
    for k in range(outer - 1):
        steps.append(
            (
                [sources[v][k] for v in range(outer)],
                [max(0, min(outer - 1, after[v][k])) for v in range(outer)],
                [int(0 <= after[v][k] < outer) for v in range(outer)],
            )
        )
    return steps


def index_of(dims, a, b, c):
    _, mid, inner = dims
    return (a * mid + b) * inner + c


def meet(peers):
    sem = pltpu.get_barrier_semaphore()
    for peer in peers:
        pl.semaphore_signal(sem, inc=1, device_id=peer, device_id_type=MESH)
    pl.semaphore_wait(sem, len(peers))


def send(src, dst, send_sem, recv_sem, peer):
    copy = pltpu.make_async_remote_copy(
        src_ref=src,
        dst_ref=dst,
        send_sem=send_sem,
        recv_sem=recv_sem,
        device_id=peer,
        device_id_type=MESH,
    )
    copy.start()
    return copy


def sent_all(ref, sem, peer):
    pltpu.make_async_remote_copy(
        src_ref=ref, dst_ref=ref, send_sem=sem, recv_sem=sem, device_id=peer, device_id_type=MESH
    ).wait_send()


def came_all(ref, sem, peer):
    pltpu.make_async_remote_copy(
        src_ref=ref, dst_ref=ref, send_sem=sem, recv_sem=sem, device_id=peer, device_id_type=MESH
    ).wait_recv()


def fetch(src, dst, sem):
    copy = pltpu.make_async_copy(src, dst, sem)
    copy.start()
    return copy


def project_stage(
    dims, n_tensor, pieces, bunch,
    inputs, vectors, base, exps, coefs, greet,
    kv_out, rows_out,
    xin, mg, vec_v, base_v, acc, hold, pout, pin,
    local_sem, keep_sem, x_send, x_recv, y_send, y_recv, g_send, g_recv, r_send, r_recv, p_send, p_recv,
):
    outer, mid, inner = dims
    group = mid * inner
    task, a, b, c = place(dims)
    y = lax.axis_index("tensor")
    mine = b * inner + c
    tasks, mats, rows, cols = vectors.shape
    row_blocks, col_blocks = exps.shape[1:3]
    tokens = inputs.shape[0]
    piece = tokens // pieces
    span = group * rows
    part = span // n_tensor
    window = 3
    turns = list(range(outer - 1, 0, -1))

    def at(a_, b_, c_):
        return {"task": index_of(dims, a_, b_, c_), "tensor": y}

    def tensor_peer(step):
        return {"task": task, "tensor": turned(y, step, n_tensor)}

    def group_peer(f, e):
        return at(a, turned(b, f, mid), turned(c, e, inner))

    def some(k):
        return slice(k * piece, (k + 1) * piece)

    def bunch_of(k):
        return slice(k * piece * bunch, (k + 1) * piece * bunch)

    base_copy = fetch(base, base_v, local_sem.at[0])
    vec_copies = [
        fetch(vectors.at[:, m], vec_v.at[:, m], local_sem.at[2 + m]) for m in range(mats)
    ]
    own_copy = fetch(
        inputs.at[:, pl.ds(pl.multiple_of(a * span, 128), span)], xin.at[a], local_sem.at[1]
    )
    greet()
    x_copies = {}
    own_cols = pl.ds(pl.multiple_of(y * part, 128), part)

    def hand_out(k):
        for d in turns:
            to = flip(a, d)
            slot = d * pieces + k
            x_copies[k, d] = send(
                inputs.at[some(k), pl.ds(pl.multiple_of(to * span + y * part, 128), part)],
                xin.at[a, some(k), own_cols],
                x_send.at[0], x_recv.at[slot], at(to, b, c),
            )

    for k in range(min(window, pieces)):
        hand_out(k)
    high = rows // row_blocks
    wide = cols // col_blocks
    base_copy.wait()
    g_copies = {}

    def share(m, f, e, hop):
        came = turned(b, -(f - hop[0]), mid) * inner + turned(c, -(e - hop[1]), inner)
        slot = (m * mid + f) * inner + e
        g_copies[m, f, e] = send(
            mg.at[came, m], mg.at[came, m], g_send.at[0], g_recv.at[slot], group_peer(*hop)
        )

    for m in range(mats):
        vec_copies[m].wait()

        def merge(i, carry):
            these = pl.ds(pl.multiple_of(i * high, 8), high)
            for j in range(col_blocks):
                across = slice(j * wide, (j + 1) * wide)
                total = base_v[m, these, across].astype(F32)
                for t in range(tasks):
                    scale = coefs[m, t] * scale_of(exps, t, m, i, j)
                    total += scale * vec_v[t, m, these, across].astype(F32)
                mg[mine, m, these, across] = total.astype(BF16)
            return carry

        lax.fori_loop(0, row_blocks, merge, 0)
        for f in range(1, mid):
            share(m, f, 0, (f, 0))
        for e in range(1, inner):
            share(m, 0, e, (0, e))

    def spread(k, d):
        a_from = flip(a, d)
        owner = a_from * group + mine
        for f in range(mid):
            for e in range(inner):
                if not (f or e):
                    continue
                to = turned(b, f, mid) * inner + turned(c, e, inner)
                send(
                    xin.at[a_from, bunch_of(k), pl.ds(pl.multiple_of(to * rows, 128), rows)],
                    rows_out.at[owner, bunch_of(k)],
                    r_send.at[0], r_recv.at[0], group_peer(f, e),
                )
        fetch(
            xin.at[a_from, bunch_of(k), pl.ds(pl.multiple_of(mine * rows, 128), rows)],
            rows_out.at[owner, bunch_of(k)],
            keep_sem.at[0],
        )

    def pass_on(k):
        for d in turns:
            x_copies[k, d].wait_recv()
        if k + window < pieces:
            hand_out(k + window)
        for d in turns:
            block = xin.at[flip(a, d), some(k), own_cols]
            for s in range(1, n_tensor):
                send(block, block, y_send.at[0], y_recv.at[k], tensor_peer(s))

    def share_on(m):
        for f in range(1, mid):
            g_copies[m, f, 0].wait_recv()
            for e in range(1, inner):
                share(m, f, e, (0, e))

    def own_part(m):
        for f in range(mid):
            for e in range(1, inner):
                g_copies[m, f, e].wait_recv()
        total = None
        for g in range(group):
            term = jnp.dot(
                xin[a, :, g * rows:(g + 1) * rows], mg[g, m], preferred_element_type=F32
            )
            total = term if total is None else total + term
        acc[m] = total

    p_copies = {}

    def p_slot(k, m, d):
        return m * (pieces + 2) + (k if d == 3 else pieces + d - 1)

    def give(k, m, d, to):
        p_copies[k, m, d] = send(
            pout.at[d, m, some(k)], pin.at[d, m, some(k)],
            p_send.at[0], p_recv.at[p_slot(k, m, d)], at(flip(a, to), b, c),
        )

    def parts(k, m):
        if not turns:
            return
        if m == 0 and n_tensor > 1:
            came_all(xin.at[:len(turns), some(k), :span - part], y_recv.at[k], tensor_peer(1))
        total = None
        for g in range(group):
            left = jnp.concatenate(
                [xin[flip(a, d), some(k), g * rows:(g + 1) * rows] for d in turns], axis=0
            )
            term = jnp.dot(left, mg[g, m], preferred_element_type=F32)
            total = term if total is None else total + term
        for n, d in enumerate(turns):
            mine_part = total[n * piece:(n + 1) * piece]
            if d == 2:
                hold[m, some(k)] = mine_part
            else:
                pout[d, m, some(k)] = mine_part.astype(BF16)
                give(k, m, d, 1)

    def combine(k, m):
        if 2 not in turns:
            return
        p_copies[k, m, 3].wait_recv()
        pout[2, m, some(k)] = (hold[m, some(k)] + pin[3, m, some(k)].astype(F32)).astype(BF16)
        give(k, m, 2, 2)

    last = pieces - 1

    def finish(m):
        total = acc[m]
        for d in turns:
            if d < 3:
                came_all(pin.at[d, m], p_recv.at[p_slot(0, m, d)], at(flip(a, d), b, c))
                total = total + pin[d, m].astype(F32)
        kv_out[m] = total.astype(BF16)

    done = {m: 0 for m in range(mats)}
    mixed = {m: 0 for m in range(mats)}
    spread_done = [0]

    def parts_to(m, count):
        while done[m] < min(count, pieces):
            parts(done[m], m)
            done[m] += 1
            while m == 0 and (spread_done[0] + 1) * bunch <= done[0]:
                for d in turns:
                    spread(spread_done[0], d)
                spread_done[0] += 1

    def combine_to(m, count):
        while mixed[m] < min(count, pieces):
            combine(mixed[m], m)
            mixed[m] += 1

    shared = set()

    def shared_up_to(m):
        for n in range(m + 1):
            if n not in shared:
                shared.add(n)
                share_on(n)
                own_part(n)

    pass_on(0)
    own_copy.wait()
    for k in range(pieces // bunch):
        spread(k, 0)
    for k in range(1, pieces):
        pass_on(k)
        if k == 1:
            shared_up_to(0)
            parts_to(0, 1)
        if k == 2:
            parts_to(0, 2)
            shared_up_to(1)
            parts_to(1, 1)
        if k == 3:
            parts_to(1, 2)
        if k == 4:
            parts_to(0, 3)
            parts_to(1, 3)
            combine_to(0, 1)
        if k == 5:
            parts_to(0, 4)
            parts_to(1, 4)
            combine_to(0, 2)
    shared_up_to(mats - 1)
    parts_to(0, pieces - 1)
    combine_to(0, 3)
    parts_to(1, pieces - 1)
    combine_to(0, 4)
    parts_to(0, pieces)
    parts_to(1, pieces)
    combine_to(0, 5)
    combine_to(1, 2)
    combine_to(0, pieces)

    def keys_ready():
        combine_to(1, pieces // 2)
        finish(0)

    def between(h, heads):
        combine_to(1, pieces // 2 + -(-(h + 1) * (pieces - pieces // 2) // heads))

    def values_ready():
        combine_to(1, pieces)
        finish(1)

    def rows_ready():
        spread_all = rows_out.at[:outer]
        pltpu.make_async_copy(spread_all, spread_all, keep_sem.at[0]).wait()
        if group > 1:
            came_all(rows_out.at[:outer * (group - 1)], r_recv.at[0], group_peer(0, 1))

    def drain():
        peer = group_peer(0, 1)
        if turns:
            sent_all(xin.at[:len(turns), :, :part], x_send.at[0], peer)
            sent_all(pout.at[1:1 + len(turns)], p_send.at[0], peer)
            if n_tensor > 1:
                sent_all(xin.at[:len(turns), :, :span - part], y_send.at[0], peer)
        if group > 1:
            sent_all(mg.at[:group - 1], g_send.at[0], peer)
            sent_all(rows_out.at[:outer * (group - 1)], r_send.at[0], peer)

    return keys_ready, between, values_ready, rows_ready, drain


def attend_stage(
    n_tensor, queries, kv, att_out, dkv_out, probs, logs, expos, outs, sums, s_send, s_recv,
    keys_ready, between, values_ready, att_done, dkv_done,
):
    task = lax.axis_index("task")
    y = lax.axis_index("tensor")
    tokens = queries.shape[0]
    heads = kv.shape[2] // HEAD
    inverse = HEAD ** (-0.5)
    peers = [{"task": task, "tensor": turned(y, s, n_tensor)} for s in range(1, n_tensor)]
    key_at = lax.broadcasted_iota(jnp.int32, (tokens, GROUP * tokens), 0)
    query_at = lax.rem(lax.broadcasted_iota(jnp.int32, (tokens, GROUP * tokens), 1), tokens)
    causal = key_at <= query_at

    def stacked(h):
        return jnp.concatenate(
            [queries[:, (h * GROUP + r) * HEAD:(h * GROUP + r + 1) * HEAD] for r in range(GROUP)],
            axis=0,
        )

    keys_ready()
    for h in range(heads):
        cut = slice(h * HEAD, (h + 1) * HEAD)
        scores = lax.dot_general(
            kv[0, :, cut], stacked(h), (((1,), (1,)), ((), ())), preferred_element_type=F32
        ) * inverse
        scores = jnp.where(causal, scores, masked_value)
        weight = jnp.exp(scores - jnp.max(scores, axis=0, keepdims=True))
        probs[h] = weight * (1.0 / jnp.sum(weight, axis=0, keepdims=True))
        between(h, heads)
    values_ready()
    total = jnp.zeros((tokens, HEAD), F32)
    moment = jnp.zeros((tokens, HEAD), F32)
    for h in range(heads):
        cut = slice(h * HEAD, (h + 1) * HEAD)
        att = lax.dot_general(
            probs[h].astype(BF16), kv[1, :, cut], (((0,), (0,)), ((), ())), preferred_element_type=F32
        ).astype(BF16)
        logits = capping * jnp.tanh(sharpen * att.astype(F32) / capping)
        expo = jnp.exp(logits)
        logs[h] = logits
        expos[h] = expo
        scaled = expo * logits
        for r in range(GROUP):
            here = slice(r * tokens, (r + 1) * tokens)
            att_out[:, (h * GROUP + r) * HEAD:(h * GROUP + r + 1) * HEAD] = att[here]
            total += expo[here]
            moment += scaled[here]
    sums[y] = jnp.concatenate(
        [
            jnp.sum(total.T, axis=0, keepdims=True),
            jnp.sum(moment.T, axis=0, keepdims=True),
            jnp.zeros((6, tokens), F32),
        ],
        axis=0,
    )
    copies = [
        send(sums.at[y], sums.at[y], s_send.at[s], s_recv.at[s], peer)
        for s, peer in enumerate(peers)
    ]
    att_done()
    for copy in copies:
        copy.wait_recv()
    whole = sums[0]
    for s in range(1, n_tensor):
        whole = whole + sums[s]
    over = 1.0 / whole[0:1]
    average = whole[1:2] * over
    entropy = jnp.sum(jnp.log(whole[0:1]) - average)
    over_col = jnp.broadcast_to(over, (HEAD, tokens)).T
    average_col = jnp.broadcast_to(average, (HEAD, tokens)).T
    over_all = jnp.concatenate([over_col] * GROUP, axis=0)
    average_all = jnp.concatenate([average_col] * GROUP, axis=0)
    for h in range(heads):
        cut = slice(h * HEAD, (h + 1) * HEAD)
        logits = logs[h]
        slope = sharpen * (1.0 - (logits / capping) ** 2)
        d_out = (slope * (-(expos[h] * over_all) * (logits - average_all))).astype(BF16)
        outs[h] = d_out
        d_values = jnp.dot(probs[h].astype(BF16), d_out, preferred_element_type=F32)
        dkv_out[1, :, cut] = d_values.astype(BF16)
    dkv_done(1)
    for h in range(heads):
        cut = slice(h * HEAD, (h + 1) * HEAD)
        prob = probs[h]
        d_probs = lax.dot_general(
            kv[1, :, cut], outs[h], (((1,), (1,)), ((), ())), preferred_element_type=F32
        )
        d_scores = (
            prob * (d_probs - jnp.sum(prob * d_probs, axis=0, keepdims=True))
        ).astype(BF16)
        d_keys = jnp.dot(d_scores, stacked(h), preferred_element_type=F32) * inverse
        dkv_out[0, :, cut] = d_keys.astype(BF16)
    dkv_done(0)
    return copies, entropy


def spread_plan(dims, mats, dkv, got, d_send, d_recv, l_send, l_recv, u_send):
    outer, mid, inner = dims
    task, a, b, c = place(dims)
    y = lax.axis_index("tensor")
    steps = line_order(outer)
    planes = [a] + [chosen(source, a) for source, _, _ in steps]
    group = mid * inner
    up = [int(v + 1 < outer) for v in range(outer)]
    down = [int(v > 0) for v in range(outer)]
    above = chosen([min(v + 1, outer - 1) for v in range(outer)], a)
    below = chosen([max(v - 1, 0) for v in range(outer)], a)
    inside = chosen([u * d for u, d in zip(up, down)], a)
    detour = outer == 4 and mid == 2
    last = 0

    def spot(plane, f, e):
        return index_of(dims, plane, turned(b, f, mid), turned(c, e, inner))

    def device(plane, f, e):
        return {"task": spot(plane, f, e), "tensor": y}

    def slot_of(m, k, f, e):
        return ((m * outer + k) * mid + f) * inner + e

    def along(m, plane, target):
        source = dkv.at[m] if plane is a else got.at[m, spot(plane, 0, 0)]
        return pltpu.make_async_remote_copy(
            src_ref=source,
            dst_ref=got.at[m, spot(plane, 0, 0)],
            send_sem=l_send.at[0],
            recv_sem=l_recv.at[m * outer + plane],
            device_id=device(target, 0, 0),
            device_id_type=MESH,
        )

    def beside(k, target, k_there):
        block = got.at[last, spot(planes[k], 1, 0)]
        return pltpu.make_async_remote_copy(
            src_ref=block,
            dst_ref=block,
            send_sem=u_send.at[0],
            recv_sem=d_recv.at[slot_of(last, k_there, 1, 0)],
            device_id=device(target, 0, 0),
            device_id_type=MESH,
        )

    def guard(copy, valid):
        @pl.when(valid == 1)
        def _():
            copy.start()

    copies = {}

    def forward(m, k, held_at, hop):
        where = index_of(
            dims, planes[k], turned(b, -held_at[0], mid), turned(c, -held_at[1], inner)
        )
        slot = (k, held_at[0] + hop[0], held_at[1] + hop[1])
        own = k == 0 and held_at == (0, 0)
        around = detour and m == last and k in (1, 3) and hop[0]
        copy = pltpu.make_async_remote_copy(
            src_ref=dkv.at[m] if own else got.at[m, where],
            dst_ref=got.at[m, where],
            send_sem=u_send.at[0] if around else d_send.at[m if detour else 0],
            recv_sem=d_recv.at[slot_of(m, *slot)],
            device_id=device(a, *hop),
            device_id_type=MESH,
        )
        copies[m, slot] = copy
        if not around:
            copy.start()
        elif k == 1:
            guard(copy, 1 - inside)

    def sent_own(m):
        if outer > 1:
            guard(along(m, a, above), chosen(up, a))
            guard(along(m, a, below), chosen(down, a))
        for f in range(1, mid):
            forward(m, 0, (0, 0), (f, 0))
        for e in range(1, inner):
            forward(m, 0, (0, 0), (0, e))

    def arrive(m, k):
        _, target, valid = steps[k - 1]
        copy = along(m, planes[k], chosen(target, a))
        copy.wait_recv()
        guard(copy, chosen(valid, a))
        for f in range(1, mid):
            forward(m, k, (0, 0), (f, 0))
        for e in range(1, inner):
            forward(m, k, (0, 0), (0, e))

    def across(m, k, f):
        copies[m, (k, f, 0)].wait_recv()
        for e in range(1, inner):
            forward(m, k, (f, 0), (0, e))
        if not detour or m != last:
            return
        if k == 0:
            guard(beside(0, chosen([1, 0, 3, 2], a), 1), 1 - inside)
        elif k != 2:
            guard(beside(k, chosen(steps[k - 1][1], a), 3), inside)

    def core(m, k, f, e):
        copies[m, (k, f, e)].wait_recv()

    def source(k, f, e):
        return index_of(dims, planes[k], turned(b, -f, mid), turned(c, -e, inner))

    def drain():
        peer = device(a, 0, 1)
        if group > 1:
            count = outer * (group - 1)
            if not detour:
                sent_all(got.at[:, :count], d_send.at[0], peer)
            for m in range(mats if detour else 0):
                kept = count - 2 if m == last else count
                sent_all(got.at[m, :kept], d_send.at[m], peer)
        if detour:
            sent_all(got.at[0, :2], u_send.at[0], peer)
        if outer > 1:
            @pl.when(inside == 1)
            def _():
                sent_all(got.at[:, :outer + 1], l_send.at[0], peer)

            @pl.when(inside == 0)
            def _():
                sent_all(got.at[:, :1], l_send.at[0], peer)

    return sent_own, arrive, across, core, source, drain


def reduce_stage(
    dims, n_tensor, groups, rows_ready, entropy, plan,
    dkv, exps, grad_out, mean_out,
    got, rows_v, vec_v, grads, helds, t_send, t_recv,
):
    outer, mid, inner = dims
    n_task = outer * mid * inner
    task, a, b, c = place(dims)
    y = lax.axis_index("tensor")
    tasks, mats, rows, cols = vec_v.shape
    row_blocks, col_blocks = exps.shape[1:3]
    _, arrive, across, core, source, drain = plan
    fresh = set()

    def take(m, k, f, e):
        own = not (k or f or e)
        if k and not (f or e):
            arrive(m, k)
        elif f and not e:
            across(m, k, f)
        elif e:
            core(m, k, f, e)
        where = source(k, f, e)
        block = dkv[m] if own else got[m, where]
        term = lax.dot_general(
            rows_v[where], block, (((0,), (0,)), ((), ())), preferred_element_type=F32
        )
        if m in fresh:
            grads[m] += term
        else:
            grads[m] = term
            fresh.add(m)

    high = rows // row_blocks
    wide = cols // col_blocks

    def contracted(m):
        def contract(i, carry):
            these = pl.ds(pl.multiple_of(i * high, 8), high)
            carry = list(carry)
            for j in range(col_blocks):
                across = slice(j * wide, (j + 1) * wide)
                grad = grads[m, these, across]
                for t in range(tasks):
                    term = grad * vec_v[t, m, these, across].astype(F32)
                    term = jnp.sum(term.reshape(high // 8, 8, wide), axis=0)
                    carry[t] = carry[t] + scale_of(exps, t, m, i, j) * term
            return tuple(carry)

        start = tuple(jnp.zeros((8, wide), F32) for _ in range(tasks))
        return lax.fori_loop(0, row_blocks, contract, start)

    rows_ready()
    lines = {}
    turns = [(k, m) for k in range(outer) for m in reversed(range(mats))]
    for step in range(len(turns) + 2):
        slots = []
        if step < len(turns):
            slots.append((turns[step], 0, 0))
        if 1 <= step <= len(turns):
            slots += [(turns[step - 1], f, 0) for f in range(1, mid)]
            slots += [(turns[step - 1], 0, e) for e in range(1, inner)]
        if step >= 2:
            slots += [(turns[step - 2], f, e) for f in range(1, mid) for e in range(1, inner)]
        for (k, m), f, e in slots:
            take(m, k, f, e)
        if step - 2 >= len(turns) - mats:
            m = turns[step - 2][1]
            lines[m] = contracted(m)
    parts = [
        jnp.sum(lines[m][t], axis=0, keepdims=True) for t in range(tasks) for m in range(mats)
    ]
    entropy = jnp.broadcast_to(entropy / (n_tensor * wide), (1, wide))
    pad = -(len(parts) + 1) % 8
    stack = jnp.concatenate(parts + [entropy, jnp.zeros((pad, wide), F32)], axis=0)
    column = jnp.sum(stack, axis=1, keepdims=True)
    shape = (stack.shape[0], helds[0].shape[2])
    along = lax.broadcasted_iota(jnp.int32, shape, 0) == lax.broadcasted_iota(jnp.int32, shape, 1)
    total = jnp.sum(jnp.where(along, column, 0.0), axis=0, keepdims=True)
    for n, (held, (slot, peers)) in enumerate(zip(helds, groups)):
        held[slot] = total
        for peer in peers:
            send(held.at[slot], held.at[slot], t_send.at[n], t_recv.at[n], peer)
        if peers:
            came_all(held.at[:len(peers)], t_recv.at[n], peers[0])
        total = held[0]
        for k in range(1, len(peers) + 1):
            total = total + held[k]
    tokens = rows_v.shape[1]
    mean_out[...] = total[0:1, tasks * mats:tasks * mats + 1] * (1.0 / (tokens * n_task))
    wide_line = jnp.broadcast_to(total[0:1], (tasks, total.shape[1]))
    spot = lax.broadcasted_iota(jnp.int32, wide_line.shape, 1)
    task_at = lax.broadcasted_iota(jnp.int32, wide_line.shape, 0)
    grid = (mats, total.shape[1])
    mat_at = lax.broadcasted_iota(jnp.int32, grid, 0)
    result = jnp.zeros(grid, F32)
    for m in range(mats):
        column = jnp.sum(jnp.where(spot == mats * task_at + m, wide_line, 0.0), axis=1, keepdims=True)
        row = jnp.sum(jnp.where(spot == task_at, column, 0.0), axis=0, keepdims=True)
        result = jnp.where(mat_at == m, row, result)
    grad_out[...] = result[:, :tasks]
    drain()
    for n, (held, (slot, peers)) in enumerate(zip(helds, groups)):
        if peers:
            sent_all(held.at[:len(peers)], t_send.at[n], peers[0])


def whole_kernel(
    dims, n_tensor, pieces, bunch,
    inputs, queries, vectors, base, exps, coefs,
    att, mean_out, grad_out,
    xin, mg, vec_v, base_v, acc, hold, pout, pin, kv, rows_v, dkv, probs, logs, expos, outs, sums,
    got, grads, q_v, att_v, io_sem, exps_v, coefs_v,
    local_sem, keep_sem, x_send, x_recv, y_send, y_recv, g_send, g_recv, r_send, r_recv, p_send, p_recv,
    s_send, s_recv, d_send, d_recv, l_send, l_recv, u_send, t_send, t_recv, *helds,
):
    n_task = dims[0] * dims[1] * dims[2]
    task = lax.axis_index("task")
    y = lax.axis_index("tensor")
    if len(helds) == 1:
        me, count = task * n_tensor + y, n_task * n_tensor
        others = [turned(me, s, count) for s in range(1, count)]
        groups = [
            (me, [{"task": k // n_tensor, "tensor": lax.rem(k, n_tensor)} for k in others]),
        ]
    else:
        groups = [
            (task, [{"task": turned(task, s, n_task), "tensor": y} for s in range(1, n_task)]),
            (y, [{"task": task, "tensor": turned(y, s, n_tensor)} for s in range(1, n_tensor)]),
        ]

    small = [fetch(exps, exps_v, io_sem.at[2]), fetch(coefs, coefs_v, io_sem.at[3])]
    waiting = []

    def greet():
        meet([peer for _, peers in groups for peer in peers])
        for copy in small:
            copy.wait()

    query_copy = fetch(queries, q_v, io_sem.at[0])
    keys_ready, between, values_ready, rows_ready, drain = project_stage(
        dims, n_tensor, pieces, bunch, inputs, vectors, base, exps_v, coefs_v, greet, kv, rows_v,
        xin, mg, vec_v, base_v, acc, hold, pout, pin,
        local_sem, keep_sem, x_send, x_recv, y_send, y_recv, g_send, g_recv, r_send, r_recv, p_send, p_recv,
    )
    query_copy.wait()
    plan = spread_plan(dims, kv.shape[0], dkv, got, d_send, d_recv, l_send, l_recv, u_send)

    def att_done():
        waiting.append(fetch(att_v, att, io_sem.at[1]))

    exchanged, entropy = attend_stage(
        n_tensor, q_v, kv, att_v, dkv, probs, logs, expos, outs, sums, s_send, s_recv,
        keys_ready, between, values_ready, att_done, plan[0],
    )
    reduce_stage(
        dims, n_tensor, groups, rows_ready, entropy, plan,
        dkv, exps_v, grad_out, mean_out,
        got, rows_v, vec_v, grads, helds, t_send, t_recv,
    )
    drain()
    for copy in exchanged:
        copy.wait_send()
    for copy in waiting:
        copy.wait()


def local(inputs, queries, task_vectors, base_weights, scale_exps, coefs):
    n_task = lax.axis_size("task")
    n_tensor = lax.axis_size("tensor")
    dims = factors(n_task)
    outer, mid, inner = dims
    group = mid * inner
    tokens = inputs.shape[0]
    tasks, mats, rows, cols = task_vectors.shape
    heads = cols // HEAD
    pieces = math.gcd(tokens // 16, 6)
    bunch = math.gcd(pieces, 2)
    hbm = pl.BlockSpec(memory_space=pltpu.HBM)
    anywhere = pl.BlockSpec(memory_space=pl.ANY)
    vmem = pl.BlockSpec(memory_space=pltpu.VMEM)
    dma = pltpu.SemaphoreType.DMA
    slots = [n_task * n_tensor] if n_task * n_tensor <= 64 else [n_task, n_tensor]

    def pair(count):
        return [dma((count,)), dma((count,))]

    attended, mean_entropy, coef_grad = pl.pallas_call(
        functools.partial(whole_kernel, dims, n_tensor, pieces, bunch),
        out_shape=(
            jax.ShapeDtypeStruct(queries.shape, BF16),
            jax.ShapeDtypeStruct((1, 1), F32),
            jax.ShapeDtypeStruct((mats, tasks), F32),
        ),
        in_specs=[hbm] * 6,
        out_specs=(anywhere, vmem, vmem),
        scratch_shapes=[
            pltpu.VMEM((outer, tokens, group * rows), BF16),
            pltpu.VMEM((group, mats, rows, cols), BF16),
            pltpu.VMEM(task_vectors.shape, BF16),
            pltpu.VMEM(base_weights.shape, BF16),
            pltpu.VMEM((mats, tokens, cols), F32),
            pltpu.VMEM((mats, tokens, cols), F32),
            pltpu.VMEM((outer, mats, tokens, cols), BF16),
            pltpu.VMEM((outer, mats, tokens, cols), BF16),
            pltpu.VMEM((mats, tokens, cols), BF16),
            pltpu.VMEM((n_task, tokens, rows), BF16),
            pltpu.VMEM((mats, tokens, cols), BF16),
            pltpu.VMEM((heads, tokens, GROUP * tokens), F32),
            pltpu.VMEM((heads, GROUP * tokens, HEAD), F32),
            pltpu.VMEM((heads, GROUP * tokens, HEAD), F32),
            pltpu.VMEM((heads, GROUP * tokens, HEAD), BF16),
            pltpu.VMEM((n_tensor, 8, tokens), F32),
            pltpu.VMEM((mats, n_task, tokens, cols), BF16),
            pltpu.VMEM((mats, rows, cols), F32),
            pltpu.VMEM(queries.shape, BF16),
            pltpu.VMEM(queries.shape, BF16),
            dma((4,)),
            pltpu.SMEM((mats, *scale_exps.shape[2:], tasks), jnp.int32), pltpu.SMEM((mats, tasks), F32),
            dma((2 + mats,)), dma((1,)),
            dma((1,)), dma((outer * pieces,)),
            dma((1,)), dma((pieces,)),
            dma((1,)), dma((mats * group,)),
            dma((1,)), dma((1,)),
            dma((1,)), dma((mats * (pieces + 2),)),
            *pair(n_tensor),
            dma((mats,)), dma((mats * n_task,)),
            dma((1,)), dma((mats * outer,)),
            dma((1,)),
            *pair(len(slots)),
            *[pltpu.VMEM((count, 1, 128), F32) for count in slots],
        ],
        compiler_params=pltpu.CompilerParams(
            collective_id=0, has_side_effects=True, vmem_limit_bytes=VMEM_BYTES
        ),
        name="whole",
    )(
        *[
            pltpu.with_memory_space_constraint(value, pltpu.HBM)
            for value in (
                inputs, queries, task_vectors, base_weights, scale_exps.transpose(1, 2, 3, 0), coefs.T
            )
        ]
    )
    return (attended, mean_entropy[0, 0], coef_grad.T)


def solution(mesh):
    return jax.shard_map(
        local,
        mesh=mesh,
        in_specs=(
            P("task", None),
            P("task", "tensor"),
            P(None, None, "task", "tensor"),
            P(None, "task", "tensor"),
            P(None, None, "task", "tensor"),
            P(),
        ),
        out_specs=(P("task", "tensor"), P(), P()),
        check_vma=False,
    )
```

```python
import functools
import math

import jax
import jax.numpy as jnp
from jax import lax
from jax.experimental import pallas as pl
from jax.experimental.pallas import tpu as pltpu
from jax.sharding import PartitionSpec as P

HEAD = 128
GROUP = 4

sharpen = 4.0
capping = 8.0
masked_value = -1e30

MESH = pl.DeviceIdType.MESH
VMEM_BYTES = 48 * 1024 * 1024
F32 = jnp.float32
BF16 = jnp.bfloat16


def factors(n_task):
    outer = math.gcd(n_task, 4)
    mid = math.gcd(n_task // outer, 2)
    return outer, mid, n_task // (outer * mid)


def place(dims):
    _, mid, inner = dims
    task = lax.axis_index("task")
    rest = lax.rem(task, mid * inner)
    return task, task // (mid * inner), rest // inner, lax.rem(rest, inner)


def turned(value, step, size):
    return lax.rem(value + (step + size), size)


def flip(value, step):
    bit = 1
    for_value = value
    while bit <= step:
        if step & bit:
            for_value = for_value + bit - 2 * bit * lax.rem(value // bit, 2)
        bit *= 2
    return for_value


def scale_of(exps, t, m, i, j):
    return lax.shift_left(jnp.int32(1), exps[m, i, j, t] + 3).astype(F32) * 0.125


def chosen(table, value):
    total = 0
    for n, entry in enumerate(table):
        if not entry:
            continue
        term, bit = entry, 1
        while bit < len(table):
            digit = lax.rem(value // bit, 2)
            term = term * (digit if n & bit else 1 - digit)
            bit *= 2
        total = total + term
    return jnp.int32(total) if isinstance(total, int) else total


def line_order(outer):
    sources = [sorted((s for s in range(outer) if s != v), key=lambda s: (abs(s - v), s if 2 * v < outer else -s)) for v in range(outer)]
    after = [[v + 1 if s < v else v - 1 for s in sources[v]] for v in range(outer)]
    steps = []
    for k in range(outer - 1):
        steps.append(
            (
                [sources[v][k] for v in range(outer)],
                [max(0, min(outer - 1, after[v][k])) for v in range(outer)],
                [int(0 <= after[v][k] < outer) for v in range(outer)],
            )
        )
    return steps


def index_of(dims, a, b, c):
    _, mid, inner = dims
    return (a * mid + b) * inner + c


def meet(peers):
    sem = pltpu.get_barrier_semaphore()
    for peer in peers:
        pl.semaphore_signal(sem, inc=1, device_id=peer, device_id_type=MESH)
    pl.semaphore_wait(sem, len(peers))


def send(src, dst, send_sem, recv_sem, peer):
    copy = pltpu.make_async_remote_copy(
        src_ref=src,
        dst_ref=dst,
        send_sem=send_sem,
        recv_sem=recv_sem,
        device_id=peer,
        device_id_type=MESH,
    )
    copy.start()
    return copy


def sent_all(ref, sem, peer):
    pltpu.make_async_remote_copy(
        src_ref=ref, dst_ref=ref, send_sem=sem, recv_sem=sem, device_id=peer, device_id_type=MESH
    ).wait_send()


def came_all(ref, sem, peer):
    pltpu.make_async_remote_copy(
        src_ref=ref, dst_ref=ref, send_sem=sem, recv_sem=sem, device_id=peer, device_id_type=MESH
    ).wait_recv()


def fetch(src, dst, sem):
    copy = pltpu.make_async_copy(src, dst, sem)
    copy.start()
    return copy


def project_stage(
    dims, n_tensor, pieces, bunch,
    inputs, vectors, base, exps, coefs, greet,
    kv_out, rows_out,
    xin, mg, vec_v, base_v, acc, hold, pout, pin,
    local_sem, keep_sem, x_send, x_recv, y_send, y_recv, g_send, g_recv, r_send, r_recv, p_send, p_recv,
):
    outer, mid, inner = dims
    group = mid * inner
    task, a, b, c = place(dims)
    y = lax.axis_index("tensor")
    mine = b * inner + c
    tasks, mats, rows, cols = vectors.shape
    row_blocks, col_blocks = exps.shape[1:3]
    tokens = inputs.shape[0]
    piece = tokens // pieces
    span = group * rows
    part = span // n_tensor
    window = 3
    turns = list(range(outer - 1, 0, -1))

    def at(a_, b_, c_):
        return {"task": index_of(dims, a_, b_, c_), "tensor": y}

    def tensor_peer(step):
        return {"task": task, "tensor": turned(y, step, n_tensor)}

    def group_peer(f, e):
        return at(a, turned(b, f, mid), turned(c, e, inner))

    def some(k):
        return slice(k * piece, (k + 1) * piece)

    def bunch_of(k):
        return slice(k * piece * bunch, (k + 1) * piece * bunch)

    base_copy = fetch(base, base_v, local_sem.at[0])
    vec_copies = [
        fetch(vectors.at[:, m], vec_v.at[:, m], local_sem.at[2 + m]) for m in range(mats)
    ]
    own_copy = fetch(
        inputs.at[:, pl.ds(pl.multiple_of(a * span, 128), span)], xin.at[a], local_sem.at[1]
    )
    greet()
    x_copies = {}
    own_cols = pl.ds(pl.multiple_of(y * part, 128), part)

    def hand_out(k):
        for d in turns:
            to = flip(a, d)
            slot = d * pieces + k
            x_copies[k, d] = send(
                inputs.at[some(k), pl.ds(pl.multiple_of(to * span + y * part, 128), part)],
                xin.at[a, some(k), own_cols],
                x_send.at[0], x_recv.at[slot], at(to, b, c),
            )

    for k in range(min(window, pieces)):
        hand_out(k)
    high = rows // row_blocks
    wide = cols // col_blocks
    base_copy.wait()
    g_copies = {}

    def share(m, f, e, hop):
        came = turned(b, -(f - hop[0]), mid) * inner + turned(c, -(e - hop[1]), inner)
        slot = (m * mid + f) * inner + e
        g_copies[m, f, e] = send(
            mg.at[came, m], mg.at[came, m], g_send.at[0], g_recv.at[slot], group_peer(*hop)
        )

    for m in range(mats):
        vec_copies[m].wait()

        def merge(i, carry):
            these = pl.ds(pl.multiple_of(i * high, 8), high)
            for j in range(col_blocks):
                across = slice(j * wide, (j + 1) * wide)
                total = base_v[m, these, across].astype(F32)
                for t in range(tasks):
                    scale = coefs[m, t] * scale_of(exps, t, m, i, j)
                    total += scale * vec_v[t, m, these, across].astype(F32)
                mg[mine, m, these, across] = total.astype(BF16)
            return carry

        lax.fori_loop(0, row_blocks, merge, 0)
        for f in range(1, mid):
            share(m, f, 0, (f, 0))
        for e in range(1, inner):
            share(m, 0, e, (0, e))

    def spread(k, d):
        a_from = flip(a, d)
        owner = a_from * group + mine
        for f in range(mid):
            for e in range(inner):
                if not (f or e):
                    continue
                to = turned(b, f, mid) * inner + turned(c, e, inner)
                send(
                    xin.at[a_from, bunch_of(k), pl.ds(pl.multiple_of(to * rows, 128), rows)],
                    rows_out.at[owner, bunch_of(k)],
                    r_send.at[0], r_recv.at[0], group_peer(f, e),
                )
        fetch(
            xin.at[a_from, bunch_of(k), pl.ds(pl.multiple_of(mine * rows, 128), rows)],
            rows_out.at[owner, bunch_of(k)],
            keep_sem.at[0],
        )

    def pass_on(k):
        for d in turns:
            x_copies[k, d].wait_recv()
        if k + window < pieces:
            hand_out(k + window)
        for d in turns:
            block = xin.at[flip(a, d), some(k), own_cols]
            for s in range(1, n_tensor):
                send(block, block, y_send.at[0], y_recv.at[k], tensor_peer(s))

    def share_on(m):
        for f in range(1, mid):
            g_copies[m, f, 0].wait_recv()
            for e in range(1, inner):
                share(m, f, e, (0, e))

    def own_part(m):
        for f in range(mid):
            for e in range(1, inner):
                g_copies[m, f, e].wait_recv()
        total = None
        for g in range(group):
            term = jnp.dot(
                xin[a, :, g * rows:(g + 1) * rows], mg[g, m], preferred_element_type=F32
            )
            total = term if total is None else total + term
        acc[m] = total

    p_copies = {}

    def p_slot(k, m, d):
        return m * (pieces + 2) + (k if d == 3 else pieces + d - 1)

    def give(k, m, d, to):
        p_copies[k, m, d] = send(
            pout.at[d, m, some(k)], pin.at[d, m, some(k)],
            p_send.at[0], p_recv.at[p_slot(k, m, d)], at(flip(a, to), b, c),
        )

    def parts(k, m):
        if not turns:
            return
        if m == 0 and n_tensor > 1:
            came_all(xin.at[:len(turns), some(k), :span - part], y_recv.at[k], tensor_peer(1))
        total = None
        for g in range(group):
            left = jnp.concatenate(
                [xin[flip(a, d), some(k), g * rows:(g + 1) * rows] for d in turns], axis=0
            )
            term = jnp.dot(left, mg[g, m], preferred_element_type=F32)
            total = term if total is None else total + term
        for n, d in enumerate(turns):
            mine_part = total[n * piece:(n + 1) * piece]
            if d == 2:
                hold[m, some(k)] = mine_part
            else:
                pout[d, m, some(k)] = mine_part.astype(BF16)
                give(k, m, d, 1)

    def combine(k, m):
        if 2 not in turns:
            return
        p_copies[k, m, 3].wait_recv()
        pout[2, m, some(k)] = (hold[m, some(k)] + pin[3, m, some(k)].astype(F32)).astype(BF16)
        give(k, m, 2, 2)

    last = pieces - 1

    def finish(m):
        total = acc[m]
        for d in turns:
            if d < 3:
                came_all(pin.at[d, m], p_recv.at[p_slot(0, m, d)], at(flip(a, d), b, c))
                total = total + pin[d, m].astype(F32)
        kv_out[m] = total.astype(BF16)

    done = {m: 0 for m in range(mats)}
    mixed = {m: 0 for m in range(mats)}
    spread_done = [0]

    def parts_to(m, count):
        while done[m] < min(count, pieces):
            parts(done[m], m)
            done[m] += 1
            while m == 0 and (spread_done[0] + 1) * bunch <= done[0]:
                for d in turns:
                    spread(spread_done[0], d)
                spread_done[0] += 1

    def combine_to(m, count):
        while mixed[m] < min(count, pieces):
            combine(mixed[m], m)
            mixed[m] += 1

    shared = set()

    def shared_up_to(m):
        for n in range(m + 1):
            if n not in shared:
                shared.add(n)
                share_on(n)
                own_part(n)

    pass_on(0)
    own_copy.wait()
    for k in range(pieces // bunch):
        spread(k, 0)
    for k in range(1, pieces):
        pass_on(k)
        if k == 1:
            shared_up_to(0)
            parts_to(0, 1)
        if k == 2:
            parts_to(0, 2)
            shared_up_to(1)
            parts_to(1, 1)
        if k == 3:
            parts_to(1, 2)
        if k >= 4:
            parts_to(0, k - 1)
            parts_to(1, k - 1)
            combine_to(0, k - 3)
    shared_up_to(mats - 1)
    parts_to(0, pieces - 1)
    combine_to(0, pieces - 3)
    parts_to(1, pieces - 1)
    combine_to(0, pieces - 2)
    parts_to(0, pieces)
    parts_to(1, pieces)
    combine_to(0, pieces - 1)
    combine_to(1, pieces - 4)
    combine_to(0, pieces)

    def keys_ready():
        combine_to(1, pieces // 2)
        finish(0)

    def between(h, heads):
        combine_to(1, pieces // 2 + -(-(h + 1) * (pieces - pieces // 2) // heads))

    def values_ready():
        combine_to(1, pieces)
        finish(1)

    def rows_ready():
        spread_all = rows_out.at[:outer]
        pltpu.make_async_copy(spread_all, spread_all, keep_sem.at[0]).wait()
        if group > 1:
            came_all(rows_out.at[:outer * (group - 1)], r_recv.at[0], group_peer(0, 1))

    def drain():
        peer = group_peer(0, 1)
        if turns:
            sent_all(xin.at[:len(turns), :, :part], x_send.at[0], peer)
            sent_all(pout.at[1:1 + len(turns)], p_send.at[0], peer)
            if n_tensor > 1:
                sent_all(xin.at[:len(turns), :, :span - part], y_send.at[0], peer)
        if group > 1:
            sent_all(mg.at[:group - 1], g_send.at[0], peer)
            sent_all(rows_out.at[:outer * (group - 1)], r_send.at[0], peer)

    return keys_ready, between, values_ready, rows_ready, drain


def attend_stage(
    n_tensor, queries, kv, att_out, dkv_out, probs, logs, expos, outs, sums, s_send, s_recv,
    keys_ready, between, values_ready, att_done, dkv_done,
):
    task = lax.axis_index("task")
    y = lax.axis_index("tensor")
    tokens = queries.shape[0]
    heads = kv.shape[2] // HEAD
    inverse = HEAD ** (-0.5)
    peers = [{"task": task, "tensor": turned(y, s, n_tensor)} for s in range(1, n_tensor)]
    key_at = lax.broadcasted_iota(jnp.int32, (tokens, GROUP * tokens), 0)
    query_at = lax.rem(lax.broadcasted_iota(jnp.int32, (tokens, GROUP * tokens), 1), tokens)
    causal = key_at <= query_at

    def stacked(h):
        return jnp.concatenate(
            [queries[:, (h * GROUP + r) * HEAD:(h * GROUP + r + 1) * HEAD] for r in range(GROUP)],
            axis=0,
        )

    keys_ready()
    for h in range(heads):
        cut = slice(h * HEAD, (h + 1) * HEAD)
        scores = lax.dot_general(
            kv[0, :, cut], stacked(h), (((1,), (1,)), ((), ())), preferred_element_type=F32
        ) * inverse
        scores = jnp.where(causal, scores, masked_value)
        weight = jnp.exp(scores - jnp.max(scores, axis=0, keepdims=True))
        probs[h] = weight * (1.0 / jnp.sum(weight, axis=0, keepdims=True))
        between(h, heads)
    values_ready()
    total = jnp.zeros((tokens, HEAD), F32)
    moment = jnp.zeros((tokens, HEAD), F32)
    for h in range(heads):
        cut = slice(h * HEAD, (h + 1) * HEAD)
        att = lax.dot_general(
            probs[h].astype(BF16), kv[1, :, cut], (((0,), (0,)), ((), ())), preferred_element_type=F32
        ).astype(BF16)
        logits = capping * jnp.tanh(sharpen * att.astype(F32) / capping)
        expo = jnp.exp(logits)
        logs[h] = logits
        expos[h] = expo
        scaled = expo * logits
        for r in range(GROUP):
            here = slice(r * tokens, (r + 1) * tokens)
            att_out[:, (h * GROUP + r) * HEAD:(h * GROUP + r + 1) * HEAD] = att[here]
            total += expo[here]
            moment += scaled[here]
    sums[y] = jnp.concatenate(
        [
            jnp.sum(total.T, axis=0, keepdims=True),
            jnp.sum(moment.T, axis=0, keepdims=True),
            jnp.zeros((6, tokens), F32),
        ],
        axis=0,
    )
    copies = [
        send(sums.at[y], sums.at[y], s_send.at[s], s_recv.at[s], peer)
        for s, peer in enumerate(peers)
    ]
    att_done()
    for copy in copies:
        copy.wait_recv()
    whole = sums[0]
    for s in range(1, n_tensor):
        whole = whole + sums[s]
    over = 1.0 / whole[0:1]
    average = whole[1:2] * over
    entropy = jnp.sum(jnp.log(whole[0:1]) - average)
    over_col = jnp.broadcast_to(over, (HEAD, tokens)).T
    average_col = jnp.broadcast_to(average, (HEAD, tokens)).T
    over_all = jnp.concatenate([over_col] * GROUP, axis=0)
    average_all = jnp.concatenate([average_col] * GROUP, axis=0)
    for h in range(heads):
        cut = slice(h * HEAD, (h + 1) * HEAD)
        logits = logs[h]
        slope = sharpen * (1.0 - (logits / capping) ** 2)
        d_out = (slope * (-(expos[h] * over_all) * (logits - average_all))).astype(BF16)
        outs[h] = d_out
        d_values = jnp.dot(probs[h].astype(BF16), d_out, preferred_element_type=F32)
        dkv_out[1, :, cut] = d_values.astype(BF16)
    dkv_done(1)
    for h in range(heads):
        cut = slice(h * HEAD, (h + 1) * HEAD)
        prob = probs[h]
        d_probs = lax.dot_general(
            kv[1, :, cut], outs[h], (((1,), (1,)), ((), ())), preferred_element_type=F32
        )
        d_scores = (
            prob * (d_probs - jnp.sum(prob * d_probs, axis=0, keepdims=True))
        ).astype(BF16)
        d_keys = jnp.dot(d_scores, stacked(h), preferred_element_type=F32) * inverse
        dkv_out[0, :, cut] = d_keys.astype(BF16)
    dkv_done(0)
    return copies, entropy


def spread_plan(dims, mats, dkv, got, d_send, d_recv, l_send, l_recv, u_send):
    outer, mid, inner = dims
    task, a, b, c = place(dims)
    y = lax.axis_index("tensor")
    steps = line_order(outer)
    planes = [a] + [chosen(source, a) for source, _, _ in steps]
    group = mid * inner
    up = [int(v + 1 < outer) for v in range(outer)]
    down = [int(v > 0) for v in range(outer)]
    above = chosen([min(v + 1, outer - 1) for v in range(outer)], a)
    below = chosen([max(v - 1, 0) for v in range(outer)], a)
    inside = chosen([u * d for u, d in zip(up, down)], a)
    detour = outer == 4 and mid == 2
    last = 0

    def spot(plane, f, e):
        return index_of(dims, plane, turned(b, f, mid), turned(c, e, inner))

    def device(plane, f, e):
        return {"task": spot(plane, f, e), "tensor": y}

    def slot_of(m, k, f, e):
        return ((m * outer + k) * mid + f) * inner + e

    def along(m, plane, target):
        source = dkv.at[m] if plane is a else got.at[m, spot(plane, 0, 0)]
        return pltpu.make_async_remote_copy(
            src_ref=source,
            dst_ref=got.at[m, spot(plane, 0, 0)],
            send_sem=l_send.at[0],
            recv_sem=l_recv.at[m * outer + plane],
            device_id=device(target, 0, 0),
            device_id_type=MESH,
        )

    def beside(k, target, k_there):
        block = got.at[last, spot(planes[k], 1, 0)]
        return pltpu.make_async_remote_copy(
            src_ref=block,
            dst_ref=block,
            send_sem=u_send.at[0],
            recv_sem=d_recv.at[slot_of(last, k_there, 1, 0)],
            device_id=device(target, 0, 0),
            device_id_type=MESH,
        )

    def guard(copy, valid):
        @pl.when(valid == 1)
        def _():
            copy.start()

    copies = {}

    def forward(m, k, held_at, hop):
        where = index_of(
            dims, planes[k], turned(b, -held_at[0], mid), turned(c, -held_at[1], inner)
        )
        slot = (k, held_at[0] + hop[0], held_at[1] + hop[1])
        own = k == 0 and held_at == (0, 0)
        around = detour and m == last and k in (1, 3) and hop[0]
        copy = pltpu.make_async_remote_copy(
            src_ref=dkv.at[m] if own else got.at[m, where],
            dst_ref=got.at[m, where],
            send_sem=u_send.at[0] if around else d_send.at[m if detour else 0],
            recv_sem=d_recv.at[slot_of(m, *slot)],
            device_id=device(a, *hop),
            device_id_type=MESH,
        )
        copies[m, slot] = copy

        def go():
            if not around:
                copy.start()
            elif k == 1:
                guard(copy, 1 - inside)

        return go

    def sent_own(m):
        if outer > 1:
            guard(along(m, a, above), chosen(up, a))
            guard(along(m, a, below), chosen(down, a))
        for f in range(1, mid):
            forward(m, 0, (0, 0), (f, 0))()
        for e in range(1, inner):
            forward(m, 0, (0, 0), (0, e))()

    def arrive(m, k, which=None):
        _, target, valid = steps[k - 1]
        copy = along(m, planes[k], chosen(target, a))
        further = chosen(valid, a)
        hops = [forward(m, k, (0, 0), (f, 0)) for f in range(1, mid)]
        hops += [forward(m, k, (0, 0), (0, e)) for e in range(1, inner)]

        def go():
            copy.wait_recv()
            guard(copy, further)
            for hop in hops:
                hop()

        if which is None:
            go()
        else:
            pl.when(inside == which)(go)

    def come(m, k):
        if k == 1:
            arrive(m, 1)
        else:
            arrive(m, k, 0)
        if k + 1 < outer:
            arrive(m, k + 1, 1)

    def across(m, k, f):
        copies[m, (k, f, 0)].wait_recv()
        for e in range(1, inner):
            forward(m, k, (f, 0), (0, e))()
        if not detour or m != last:
            return
        if k == 0:
            guard(beside(0, chosen([1, 0, 3, 2], a), 1), 1 - inside)
        elif k != 2:
            guard(beside(k, chosen(steps[k - 1][1], a), 3), inside)

    def core(m, k, f, e):
        copies[m, (k, f, e)].wait_recv()

    def source(k, f, e):
        return index_of(dims, planes[k], turned(b, -f, mid), turned(c, -e, inner))

    def drain():
        peer = device(a, 0, 1)
        if group > 1:
            count = outer * (group - 1)
            if not detour:
                sent_all(got.at[:, :count], d_send.at[0], peer)
            for m in range(mats if detour else 0):
                kept = count - 2 if m == last else count
                sent_all(got.at[m, :kept], d_send.at[m], peer)
        if detour:
            sent_all(got.at[0, :2], u_send.at[0], peer)
        if outer > 1:
            @pl.when(inside == 1)
            def _():
                sent_all(got.at[:, :outer + 1], l_send.at[0], peer)

            @pl.when(inside == 0)
            def _():
                sent_all(got.at[:, :1], l_send.at[0], peer)

    return sent_own, come, across, core, source, drain


def reduce_stage(
    dims, n_tensor, groups, rows_ready, entropy, plan,
    dkv, exps, grad_out, mean_out,
    got, rows_v, vec_v, grads, helds, t_send, t_recv,
):
    outer, mid, inner = dims
    n_task = outer * mid * inner
    task, a, b, c = place(dims)
    y = lax.axis_index("tensor")
    tasks, mats, rows, cols = vec_v.shape
    row_blocks, col_blocks = exps.shape[1:3]
    _, come, across, core, source, drain = plan
    fresh = set()

    def take(m, k, f, e):
        own = not (k or f or e)
        if k and not (f or e):
            come(m, k)
        elif f and not e:
            across(m, k, f)
        elif e:
            core(m, k, f, e)
        where = source(k, f, e)
        block = dkv[m] if own else got[m, where]
        term = lax.dot_general(
            rows_v[where], block, (((0,), (0,)), ((), ())), preferred_element_type=F32
        )
        if m in fresh:
            grads[m] += term
        else:
            grads[m] = term
            fresh.add(m)

    high = rows // row_blocks
    wide = cols // col_blocks

    def contracted(m):
        def contract(i, carry):
            these = pl.ds(pl.multiple_of(i * high, 8), high)
            carry = list(carry)
            for j in range(col_blocks):
                across = slice(j * wide, (j + 1) * wide)
                grad = grads[m, these, across]
                for t in range(tasks):
                    term = grad * vec_v[t, m, these, across].astype(F32)
                    term = jnp.sum(term.reshape(high // 8, 8, wide), axis=0)
                    carry[t] = carry[t] + scale_of(exps, t, m, i, j) * term
            return tuple(carry)

        start = tuple(jnp.zeros((8, wide), F32) for _ in range(tasks))
        return lax.fori_loop(0, row_blocks, contract, start)

    rows_ready()
    lines = {}
    turns = [(k, m) for k in range(outer) for m in reversed(range(mats))]
    across_turns = turns[:-mats] + turns[-mats:][::-1]
    for step in range(len(turns) + 2):
        slots = []
        if step < len(turns):
            slots.append((turns[step], 0, 0))
        if 1 <= step <= len(turns):
            slots += [(across_turns[step - 1], f, 0) for f in range(1, mid)]
            slots += [(turns[step - 1], 0, e) for e in range(1, inner)]
        if step >= 2:
            slots += [(across_turns[step - 2], f, e) for f in range(1, mid) for e in range(1, inner)]
        for (k, m), f, e in slots:
            take(m, k, f, e)
        if step - 2 >= len(turns) - mats:
            m = across_turns[step - 2][1]
            lines[m] = contracted(m)
    parts = [
        jnp.sum(lines[m][t], axis=0, keepdims=True) for t in range(tasks) for m in range(mats)
    ]
    entropy = jnp.broadcast_to(entropy / (n_tensor * wide), (1, wide))
    pad = -(len(parts) + 1) % 8
    stack = jnp.concatenate(parts + [entropy, jnp.zeros((pad, wide), F32)], axis=0)
    column = jnp.sum(stack, axis=1, keepdims=True)
    shape = (stack.shape[0], helds[0].shape[2])
    along = lax.broadcasted_iota(jnp.int32, shape, 0) == lax.broadcasted_iota(jnp.int32, shape, 1)
    total = jnp.sum(jnp.where(along, column, 0.0), axis=0, keepdims=True)
    for n, (held, (slot, peers)) in enumerate(zip(helds, groups)):
        held[slot] = total
        for peer in peers:
            send(held.at[slot], held.at[slot], t_send.at[n], t_recv.at[n], peer)
        if peers:
            came_all(held.at[:len(peers)], t_recv.at[n], peers[0])
        total = held[0]
        for k in range(1, len(peers) + 1):
            total = total + held[k]
    tokens = rows_v.shape[1]
    mean_out[...] = total[0:1, tasks * mats:tasks * mats + 1] * (1.0 / (tokens * n_task))
    wide_line = jnp.broadcast_to(total[0:1], (tasks, total.shape[1]))
    spot = lax.broadcasted_iota(jnp.int32, wide_line.shape, 1)
    task_at = lax.broadcasted_iota(jnp.int32, wide_line.shape, 0)
    grid = (mats, total.shape[1])
    mat_at = lax.broadcasted_iota(jnp.int32, grid, 0)
    result = jnp.zeros(grid, F32)
    for m in range(mats):
        column = jnp.sum(jnp.where(spot == mats * task_at + m, wide_line, 0.0), axis=1, keepdims=True)
        row = jnp.sum(jnp.where(spot == task_at, column, 0.0), axis=0, keepdims=True)
        result = jnp.where(mat_at == m, row, result)
    grad_out[...] = result[:, :tasks]
    drain()
    for n, (held, (slot, peers)) in enumerate(zip(helds, groups)):
        if peers:
            sent_all(held.at[:len(peers)], t_send.at[n], peers[0])


def whole_kernel(
    dims, n_tensor, pieces, bunch,
    inputs, queries, vectors, base, exps, coefs,
    att, mean_out, grad_out,
    xin, mg, vec_v, base_v, acc, hold, pout, pin, kv, rows_v, dkv, probs, logs, expos, outs, sums,
    got, grads, q_v, att_v, io_sem, exps_v, coefs_v,
    local_sem, keep_sem, x_send, x_recv, y_send, y_recv, g_send, g_recv, r_send, r_recv, p_send, p_recv,
    s_send, s_recv, d_send, d_recv, l_send, l_recv, u_send, t_send, t_recv, *helds,
):
    n_task = dims[0] * dims[1] * dims[2]
    task = lax.axis_index("task")
    y = lax.axis_index("tensor")
    if len(helds) == 1:
        me, count = task * n_tensor + y, n_task * n_tensor
        others = [turned(me, s, count) for s in range(1, count)]
        groups = [
            (me, [{"task": k // n_tensor, "tensor": lax.rem(k, n_tensor)} for k in others]),
        ]
    else:
        groups = [
            (task, [{"task": turned(task, s, n_task), "tensor": y} for s in range(1, n_task)]),
            (y, [{"task": task, "tensor": turned(y, s, n_tensor)} for s in range(1, n_tensor)]),
        ]

    small = [fetch(exps, exps_v, io_sem.at[2]), fetch(coefs, coefs_v, io_sem.at[3])]
    waiting = []

    def greet():
        meet([peer for _, peers in groups for peer in peers])
        for copy in small:
            copy.wait()

    query_copy = fetch(queries, q_v, io_sem.at[0])
    keys_ready, between, values_ready, rows_ready, drain = project_stage(
        dims, n_tensor, pieces, bunch, inputs, vectors, base, exps_v, coefs_v, greet, kv, rows_v,
        xin, mg, vec_v, base_v, acc, hold, pout, pin,
        local_sem, keep_sem, x_send, x_recv, y_send, y_recv, g_send, g_recv, r_send, r_recv, p_send, p_recv,
    )
    query_copy.wait()
    plan = spread_plan(dims, kv.shape[0], dkv, got, d_send, d_recv, l_send, l_recv, u_send)

    def att_done():
        waiting.append(fetch(att_v, att, io_sem.at[1]))

    exchanged, entropy = attend_stage(
        n_tensor, q_v, kv, att_v, dkv, probs, logs, expos, outs, sums, s_send, s_recv,
        keys_ready, between, values_ready, att_done, plan[0],
    )
    reduce_stage(
        dims, n_tensor, groups, rows_ready, entropy, plan,
        dkv, exps_v, grad_out, mean_out,
        got, rows_v, vec_v, grads, helds, t_send, t_recv,
    )
    drain()
    for copy in exchanged:
        copy.wait_send()
    for copy in waiting:
        copy.wait()


def local(inputs, queries, task_vectors, base_weights, scale_exps, coefs):
    n_task = lax.axis_size("task")
    n_tensor = lax.axis_size("tensor")
    dims = factors(n_task)
    outer, mid, inner = dims
    group = mid * inner
    tokens = inputs.shape[0]
    tasks, mats, rows, cols = task_vectors.shape
    heads = cols // HEAD
    pieces = math.gcd(tokens // 16, 6)
    bunch = math.gcd(pieces, 2)
    hbm = pl.BlockSpec(memory_space=pltpu.HBM)
    anywhere = pl.BlockSpec(memory_space=pl.ANY)
    vmem = pl.BlockSpec(memory_space=pltpu.VMEM)
    dma = pltpu.SemaphoreType.DMA
    slots = [n_task * n_tensor] if n_task * n_tensor <= 64 else [n_task, n_tensor]

    def pair(count):
        return [dma((count,)), dma((count,))]

    attended, mean_entropy, coef_grad = pl.pallas_call(
        functools.partial(whole_kernel, dims, n_tensor, pieces, bunch),
        out_shape=(
            jax.ShapeDtypeStruct(queries.shape, BF16),
            jax.ShapeDtypeStruct((1, 1), F32),
            jax.ShapeDtypeStruct((mats, tasks), F32),
        ),
        in_specs=[hbm] * 6,
        out_specs=(anywhere, vmem, vmem),
        scratch_shapes=[
            pltpu.VMEM((outer, tokens, group * rows), BF16),
            pltpu.VMEM((group, mats, rows, cols), BF16),
            pltpu.VMEM(task_vectors.shape, BF16),
            pltpu.VMEM(base_weights.shape, BF16),
            pltpu.VMEM((mats, tokens, cols), F32),
            pltpu.VMEM((mats, tokens, cols), F32),
            pltpu.VMEM((outer, mats, tokens, cols), BF16),
            pltpu.VMEM((outer, mats, tokens, cols), BF16),
            pltpu.VMEM((mats, tokens, cols), BF16),
            pltpu.VMEM((n_task, tokens, rows), BF16),
            pltpu.VMEM((mats, tokens, cols), BF16),
            pltpu.VMEM((heads, tokens, GROUP * tokens), F32),
            pltpu.VMEM((heads, GROUP * tokens, HEAD), F32),
            pltpu.VMEM((heads, GROUP * tokens, HEAD), F32),
            pltpu.VMEM((heads, GROUP * tokens, HEAD), BF16),
            pltpu.VMEM((n_tensor, 8, tokens), F32),
            pltpu.VMEM((mats, n_task, tokens, cols), BF16),
            pltpu.VMEM((mats, rows, cols), F32),
            pltpu.VMEM(queries.shape, BF16),
            pltpu.VMEM(queries.shape, BF16),
            dma((4,)),
            pltpu.SMEM((mats, *scale_exps.shape[2:], tasks), jnp.int32), pltpu.SMEM((mats, tasks), F32),
            dma((2 + mats,)), dma((1,)),
            dma((1,)), dma((outer * pieces,)),
            dma((1,)), dma((pieces,)),
            dma((1,)), dma((mats * group,)),
            dma((1,)), dma((1,)),
            dma((1,)), dma((mats * (pieces + 2),)),
            *pair(n_tensor),
            dma((mats,)), dma((mats * n_task,)),
            dma((1,)), dma((mats * outer,)),
            dma((1,)),
            *pair(len(slots)),
            *[pltpu.VMEM((count, 1, 128), F32) for count in slots],
        ],
        compiler_params=pltpu.CompilerParams(
            collective_id=0, has_side_effects=True, vmem_limit_bytes=VMEM_BYTES
        ),
        name="whole",
    )(
        *[
            pltpu.with_memory_space_constraint(value, pltpu.HBM)
            for value in (
                inputs, queries, task_vectors, base_weights, scale_exps.transpose(1, 2, 3, 0), coefs.T
            )
        ]
    )
    return (attended, mean_entropy[0, 0], coef_grad.T)


def solution(mesh):
    return jax.shard_map(
        local,
        mesh=mesh,
        in_specs=(
            P("task", None),
            P("task", "tensor"),
            P(None, None, "task", "tensor"),
            P(None, "task", "tensor"),
            P(None, None, "task", "tensor"),
            P(),
        ),
        out_specs=(P("task", "tensor"), P(), P()),
        check_vma=False,
    )
```

```python
import functools
import math

import jax
import jax.numpy as jnp
from jax import lax
from jax.experimental import pallas as pl
from jax.experimental.pallas import tpu as pltpu
from jax.sharding import PartitionSpec as P

HEAD = 128
GROUP = 4

sharpen = 4.0
capping = 8.0
masked_value = -1e30

MESH = pl.DeviceIdType.MESH
VMEM_BYTES = 48 * 1024 * 1024
F32 = jnp.float32
BF16 = jnp.bfloat16


def factors(n_task):
    outer = math.gcd(n_task, 4)
    mid = math.gcd(n_task // outer, 2)
    return outer, mid, n_task // (outer * mid)


def place(dims):
    _, mid, inner = dims
    task = lax.axis_index("task")
    rest = lax.rem(task, mid * inner)
    return task, task // (mid * inner), rest // inner, lax.rem(rest, inner)


def turned(value, step, size):
    return lax.rem(value + (step + size), size)


def flip(value, step):
    bit = 1
    for_value = value
    while bit <= step:
        if step & bit:
            for_value = for_value + bit - 2 * bit * lax.rem(value // bit, 2)
        bit *= 2
    return for_value


def scale_of(exps, t, m, i, j):
    return lax.shift_left(jnp.int32(1), exps[m, i, j, t] + 3).astype(F32) * 0.125


def chosen(table, value):
    total = 0
    for n, entry in enumerate(table):
        if not entry:
            continue
        term, bit = entry, 1
        while bit < len(table):
            digit = lax.rem(value // bit, 2)
            term = term * (digit if n & bit else 1 - digit)
            bit *= 2
        total = total + term
    return jnp.int32(total) if isinstance(total, int) else total


def line_order(outer):
    sources = [sorted((s for s in range(outer) if s != v), key=lambda s: (abs(s - v), s if 2 * v < outer else -s)) for v in range(outer)]
    after = [[v + 1 if s < v else v - 1 for s in sources[v]] for v in range(outer)]
    steps = []
    for k in range(outer - 1):
        steps.append(
            (
                [sources[v][k] for v in range(outer)],
                [max(0, min(outer - 1, after[v][k])) for v in range(outer)],
                [int(0 <= after[v][k] < outer) for v in range(outer)],
            )
        )
    return steps


def index_of(dims, a, b, c):
    _, mid, inner = dims
    return (a * mid + b) * inner + c


def meet(peers):
    sem = pltpu.get_barrier_semaphore()
    for peer in peers:
        pl.semaphore_signal(sem, inc=1, device_id=peer, device_id_type=MESH)
    pl.semaphore_wait(sem, len(peers))


def send(src, dst, send_sem, recv_sem, peer):
    copy = pltpu.make_async_remote_copy(
        src_ref=src,
        dst_ref=dst,
        send_sem=send_sem,
        recv_sem=recv_sem,
        device_id=peer,
        device_id_type=MESH,
    )
    copy.start()
    return copy


def sent_all(ref, sem, peer):
    pltpu.make_async_remote_copy(
        src_ref=ref, dst_ref=ref, send_sem=sem, recv_sem=sem, device_id=peer, device_id_type=MESH
    ).wait_send()


def came_all(ref, sem, peer):
    pltpu.make_async_remote_copy(
        src_ref=ref, dst_ref=ref, send_sem=sem, recv_sem=sem, device_id=peer, device_id_type=MESH
    ).wait_recv()


def fetch(src, dst, sem):
    copy = pltpu.make_async_copy(src, dst, sem)
    copy.start()
    return copy


def project_stage(
    dims, n_tensor, pieces, bunch,
    inputs, vectors, base, exps, coefs, greet,
    kv_out, rows_out,
    xin, mg, vec_v, base_v, acc, hold, pout, pin,
    local_sem, keep_sem, x_send, x_recv, y_send, y_recv, g_send, g_recv, r_send, r_recv, p_send, p_recv,
):
    outer, mid, inner = dims
    group = mid * inner
    task, a, b, c = place(dims)
    y = lax.axis_index("tensor")
    mine = b * inner + c
    tasks, mats, rows, cols = vectors.shape
    row_blocks, col_blocks = exps.shape[1:3]
    tokens = inputs.shape[0]
    piece = tokens // pieces
    span = group * rows
    part = span // n_tensor
    window = 3
    turns = list(range(outer - 1, 0, -1))

    def at(a_, b_, c_):
        return {"task": index_of(dims, a_, b_, c_), "tensor": y}

    def tensor_peer(step):
        return {"task": task, "tensor": turned(y, step, n_tensor)}

    def group_peer(f, e):
        return at(a, turned(b, f, mid), turned(c, e, inner))

    def some(k):
        return slice(k * piece, (k + 1) * piece)

    def bunch_of(k):
        return slice(k * piece * bunch, (k + 1) * piece * bunch)

    base_copy = fetch(base, base_v, local_sem.at[0])
    vec_copies = [
        fetch(vectors.at[:, m], vec_v.at[:, m], local_sem.at[2 + m]) for m in range(mats)
    ]
    own_copy = fetch(
        inputs.at[:, pl.ds(pl.multiple_of(a * span, 128), span)], xin.at[a], local_sem.at[1]
    )
    greet()
    x_copies = {}
    own_cols = pl.ds(pl.multiple_of(y * part, 128), part)

    def hand_out(k):
        for d in turns:
            to = flip(a, d)
            slot = d * pieces + k
            x_copies[k, d] = send(
                inputs.at[some(k), pl.ds(pl.multiple_of(to * span + y * part, 128), part)],
                xin.at[a, some(k), own_cols],
                x_send.at[0], x_recv.at[slot], at(to, b, c),
            )

    for k in range(min(window, pieces)):
        hand_out(k)
    high = rows // row_blocks
    wide = cols // col_blocks
    base_copy.wait()
    g_copies = {}

    def share(m, f, e, hop):
        came = turned(b, -(f - hop[0]), mid) * inner + turned(c, -(e - hop[1]), inner)
        slot = (m * mid + f) * inner + e
        g_copies[m, f, e] = send(
            mg.at[came, m], mg.at[came, m], g_send.at[0], g_recv.at[slot], group_peer(*hop)
        )

    for m in range(mats):
        vec_copies[m].wait()

        def merge(i, carry):
            these = pl.ds(pl.multiple_of(i * high, 8), high)
            for j in range(col_blocks):
                across = slice(j * wide, (j + 1) * wide)
                total = base_v[m, these, across].astype(F32)
                for t in range(tasks):
                    scale = coefs[m, t] * scale_of(exps, t, m, i, j)
                    total += scale * vec_v[t, m, these, across].astype(F32)
                mg[mine, m, these, across] = total.astype(BF16)
            return carry

        lax.fori_loop(0, row_blocks, merge, 0)
        for f in range(1, mid):
            share(m, f, 0, (f, 0))
        for e in range(1, inner):
            share(m, 0, e, (0, e))

    def spread(k, d):
        a_from = flip(a, d)
        owner = a_from * group + mine
        for f in range(mid):
            for e in range(inner):
                if not (f or e):
                    continue
                to = turned(b, f, mid) * inner + turned(c, e, inner)
                send(
                    xin.at[a_from, bunch_of(k), pl.ds(pl.multiple_of(to * rows, 128), rows)],
                    rows_out.at[owner, bunch_of(k)],
                    r_send.at[0], r_recv.at[0], group_peer(f, e),
                )
        fetch(
            xin.at[a_from, bunch_of(k), pl.ds(pl.multiple_of(mine * rows, 128), rows)],
            rows_out.at[owner, bunch_of(k)],
            keep_sem.at[0],
        )

    def pass_on(k):
        for d in turns:
            x_copies[k, d].wait_recv()
        if k + window < pieces:
            hand_out(k + window)
        for d in turns:
            block = xin.at[flip(a, d), some(k), own_cols]
            for s in range(1, n_tensor):
                send(block, block, y_send.at[0], y_recv.at[k], tensor_peer(s))

    def share_on(m):
        for f in range(1, mid):
            g_copies[m, f, 0].wait_recv()
            for e in range(1, inner):
                share(m, f, e, (0, e))

    def own_part(m):
        for f in range(mid):
            for e in range(1, inner):
                g_copies[m, f, e].wait_recv()
        total = None
        for g in range(group):
            term = jnp.dot(
                xin[a, :, g * rows:(g + 1) * rows], mg[g, m], preferred_element_type=F32
            )
            total = term if total is None else total + term
        acc[m] = total

    p_copies = {}

    def p_slot(k, m, d):
        return m * (pieces + 2) + (k if d == 3 else pieces + d - 1)

    def give(k, m, d, to):
        p_copies[k, m, d] = send(
            pout.at[d, m, some(k)], pin.at[d, m, some(k)],
            p_send.at[0], p_recv.at[p_slot(k, m, d)], at(flip(a, to), b, c),
        )

    def parts(k, m):
        if not turns:
            return
        if m == 0 and n_tensor > 1:
            came_all(xin.at[:len(turns), some(k), :span - part], y_recv.at[k], tensor_peer(1))
        total = None
        for g in range(group):
            left = jnp.concatenate(
                [xin[flip(a, d), some(k), g * rows:(g + 1) * rows] for d in turns], axis=0
            )
            term = jnp.dot(left, mg[g, m], preferred_element_type=F32)
            total = term if total is None else total + term
        for n, d in enumerate(turns):
            mine_part = total[n * piece:(n + 1) * piece]
            if d == 2:
                hold[m, some(k)] = mine_part
            else:
                pout[d, m, some(k)] = mine_part.astype(BF16)
                give(k, m, d, 1)

    def combine(k, m):
        if 2 not in turns:
            return
        p_copies[k, m, 3].wait_recv()
        pout[2, m, some(k)] = (hold[m, some(k)] + pin[3, m, some(k)].astype(F32)).astype(BF16)
        give(k, m, 2, 2)

    last = pieces - 1

    def finish(m):
        total = acc[m]
        for d in turns:
            if d < 3:
                came_all(pin.at[d, m], p_recv.at[p_slot(0, m, d)], at(flip(a, d), b, c))
                total = total + pin[d, m].astype(F32)
        kv_out[m] = total.astype(BF16)

    done = {m: 0 for m in range(mats)}
    mixed = {m: 0 for m in range(mats)}
    spread_done = [0]

    def parts_to(m, count):
        while done[m] < min(count, pieces):
            parts(done[m], m)
            done[m] += 1
            while m == 0 and (spread_done[0] + 1) * bunch <= done[0]:
                for d in turns:
                    spread(spread_done[0], d)
                spread_done[0] += 1

    def combine_to(m, count):
        while mixed[m] < min(count, pieces):
            combine(mixed[m], m)
            mixed[m] += 1

    shared = set()

    def shared_up_to(m):
        for n in range(m + 1):
            if n not in shared:
                shared.add(n)
                share_on(n)
                own_part(n)

    pass_on(0)
    own_copy.wait()
    for k in range(pieces // bunch):
        spread(k, 0)
    for k in range(1, pieces):
        pass_on(k)
        if k == 1:
            shared_up_to(0)
            parts_to(0, 1)
        if k == 2:
            parts_to(0, 2)
            shared_up_to(1)
            parts_to(1, 1)
        if k == 3:
            parts_to(1, 2)
        if k >= 4:
            parts_to(0, k - 1)
            parts_to(1, k - 1)
            combine_to(0, k - 3)
    shared_up_to(mats - 1)
    parts_to(0, pieces - 1)
    combine_to(0, pieces - 3)
    parts_to(1, pieces - 1)
    combine_to(0, pieces - 2)
    parts_to(0, pieces)
    parts_to(1, pieces)
    combine_to(0, pieces - 1)
    combine_to(1, pieces - 4)
    combine_to(0, pieces)

    def keys_ready():
        combine_to(1, pieces // 2)
        finish(0)

    def between(h, heads):
        combine_to(1, pieces // 2 + -(-(h + 1) * (pieces - pieces // 2) // heads))

    def values_ready():
        combine_to(1, pieces)
        finish(1)

    def rows_ready():
        spread_all = rows_out.at[:outer]
        pltpu.make_async_copy(spread_all, spread_all, keep_sem.at[0]).wait()
        if group > 1:
            came_all(rows_out.at[:outer * (group - 1)], r_recv.at[0], group_peer(0, 1))

    def drain():
        peer = group_peer(0, 1)
        if turns:
            sent_all(xin.at[:len(turns), :, :part], x_send.at[0], peer)
            sent_all(pout.at[1:1 + len(turns)], p_send.at[0], peer)
            if n_tensor > 1:
                sent_all(xin.at[:len(turns), :, :span - part], y_send.at[0], peer)
        if group > 1:
            sent_all(mg.at[:group - 1], g_send.at[0], peer)
            sent_all(rows_out.at[:outer * (group - 1)], r_send.at[0], peer)

    return keys_ready, between, values_ready, rows_ready, drain


def attend_stage(
    n_tensor, queries, kv, att_out, dkv_out, probs, logs, expos, outs, sums, s_send, s_recv,
    keys_ready, between, values_ready, att_done, dkv_done,
):
    task = lax.axis_index("task")
    y = lax.axis_index("tensor")
    tokens = queries.shape[0]
    heads = kv.shape[2] // HEAD
    inverse = HEAD ** (-0.5)
    peers = [{"task": task, "tensor": turned(y, s, n_tensor)} for s in range(1, n_tensor)]
    key_at = lax.broadcasted_iota(jnp.int32, (tokens, GROUP * tokens), 0)
    query_at = lax.rem(lax.broadcasted_iota(jnp.int32, (tokens, GROUP * tokens), 1), tokens)
    causal = key_at <= query_at

    def stacked(h):
        return jnp.concatenate(
            [queries[:, (h * GROUP + r) * HEAD:(h * GROUP + r + 1) * HEAD] for r in range(GROUP)],
            axis=0,
        )

    keys_ready()
    for h in range(heads):
        cut = slice(h * HEAD, (h + 1) * HEAD)
        scores = lax.dot_general(
            kv[0, :, cut], stacked(h), (((1,), (1,)), ((), ())), preferred_element_type=F32
        ) * inverse
        scores = jnp.where(causal, scores, masked_value)
        weight = jnp.exp(scores - jnp.max(scores, axis=0, keepdims=True))
        probs[h] = weight * (1.0 / jnp.sum(weight, axis=0, keepdims=True))
        between(h, heads)
    values_ready()
    total = jnp.zeros((tokens, HEAD), F32)
    moment = jnp.zeros((tokens, HEAD), F32)
    for h in range(heads):
        cut = slice(h * HEAD, (h + 1) * HEAD)
        att = lax.dot_general(
            probs[h].astype(BF16), kv[1, :, cut], (((0,), (0,)), ((), ())), preferred_element_type=F32
        ).astype(BF16)
        logits = capping * jnp.tanh(sharpen * att.astype(F32) / capping)
        expo = jnp.exp(logits)
        logs[h] = logits
        expos[h] = expo
        scaled = expo * logits
        for r in range(GROUP):
            here = slice(r * tokens, (r + 1) * tokens)
            att_out[:, (h * GROUP + r) * HEAD:(h * GROUP + r + 1) * HEAD] = att[here]
            total += expo[here]
            moment += scaled[here]
    sums[y] = jnp.concatenate(
        [
            jnp.sum(total.T, axis=0, keepdims=True),
            jnp.sum(moment.T, axis=0, keepdims=True),
            jnp.zeros((6, tokens), F32),
        ],
        axis=0,
    )
    copies = [
        send(sums.at[y], sums.at[y], s_send.at[s], s_recv.at[s], peer)
        for s, peer in enumerate(peers)
    ]
    att_done()
    for copy in copies:
        copy.wait_recv()
    whole = sums[0]
    for s in range(1, n_tensor):
        whole = whole + sums[s]
    over = 1.0 / whole[0:1]
    average = whole[1:2] * over
    entropy = jnp.sum(jnp.log(whole[0:1]) - average)
    over_col = jnp.broadcast_to(over, (HEAD, tokens)).T
    average_col = jnp.broadcast_to(average, (HEAD, tokens)).T
    over_all = jnp.concatenate([over_col] * GROUP, axis=0)
    average_all = jnp.concatenate([average_col] * GROUP, axis=0)
    for h in range(heads):
        cut = slice(h * HEAD, (h + 1) * HEAD)
        logits = logs[h]
        slope = sharpen * (1.0 - (logits / capping) ** 2)
        d_out = (slope * (-(expos[h] * over_all) * (logits - average_all))).astype(BF16)
        outs[h] = d_out
        d_values = jnp.dot(probs[h].astype(BF16), d_out, preferred_element_type=F32)
        dkv_out[1, :, cut] = d_values.astype(BF16)
    dkv_done(1)
    for h in range(heads):
        cut = slice(h * HEAD, (h + 1) * HEAD)
        prob = probs[h]
        d_probs = lax.dot_general(
            kv[1, :, cut], outs[h], (((1,), (1,)), ((), ())), preferred_element_type=F32
        )
        d_scores = (
            prob * (d_probs - jnp.sum(prob * d_probs, axis=0, keepdims=True))
        ).astype(BF16)
        d_keys = jnp.dot(d_scores, stacked(h), preferred_element_type=F32) * inverse
        dkv_out[0, :, cut] = d_keys.astype(BF16)
    dkv_done(0)
    return copies, entropy


def spread_plan(dims, mats, dkv, got, d_send, d_recv, l_send, l_recv, u_send):
    outer, mid, inner = dims
    task, a, b, c = place(dims)
    y = lax.axis_index("tensor")
    steps = line_order(outer)
    planes = [a] + [chosen(source, a) for source, _, _ in steps]
    group = mid * inner
    up = [int(v + 1 < outer) for v in range(outer)]
    down = [int(v > 0) for v in range(outer)]
    above = chosen([min(v + 1, outer - 1) for v in range(outer)], a)
    below = chosen([max(v - 1, 0) for v in range(outer)], a)
    inside = chosen([u * d for u, d in zip(up, down)], a)
    detour = outer == 4 and mid == 2
    last = 0

    def spot(plane, f, e):
        return index_of(dims, plane, turned(b, f, mid), turned(c, e, inner))

    def device(plane, f, e):
        return {"task": spot(plane, f, e), "tensor": y}

    def slot_of(m, k, f, e):
        return ((m * outer + k) * mid + f) * inner + e

    def along(m, plane, target):
        source = dkv.at[m] if plane is a else got.at[m, spot(plane, 0, 0)]
        return pltpu.make_async_remote_copy(
            src_ref=source,
            dst_ref=got.at[m, spot(plane, 0, 0)],
            send_sem=l_send.at[0],
            recv_sem=l_recv.at[m * outer + plane],
            device_id=device(target, 0, 0),
            device_id_type=MESH,
        )

    def beside(k, target, k_there):
        block = got.at[last, spot(planes[k], 1, 0)]
        return pltpu.make_async_remote_copy(
            src_ref=block,
            dst_ref=block,
            send_sem=u_send.at[0],
            recv_sem=d_recv.at[slot_of(last, k_there, 1, 0)],
            device_id=device(target, 0, 0),
            device_id_type=MESH,
        )

    def guard(copy, valid):
        @pl.when(valid == 1)
        def _():
            copy.start()

    copies = {}

    def forward(m, k, held_at, hop):
        where = index_of(
            dims, planes[k], turned(b, -held_at[0], mid), turned(c, -held_at[1], inner)
        )
        slot = (k, held_at[0] + hop[0], held_at[1] + hop[1])
        own = k == 0 and held_at == (0, 0)
        around = detour and m == last and k in (1, 3) and hop[0]
        copy = pltpu.make_async_remote_copy(
            src_ref=dkv.at[m] if own else got.at[m, where],
            dst_ref=got.at[m, where],
            send_sem=u_send.at[0] if around else d_send.at[m if detour else 0],
            recv_sem=d_recv.at[slot_of(m, *slot)],
            device_id=device(a, *hop),
            device_id_type=MESH,
        )
        copies[m, slot] = copy

        def go():
            if not around:
                copy.start()
            elif k == 1:
                guard(copy, 1 - inside)

        return go

    def sent_own(m):
        if outer > 1:
            guard(along(m, a, above), chosen(up, a))
            guard(along(m, a, below), chosen(down, a))
        for f in range(1, mid):
            forward(m, 0, (0, 0), (f, 0))()
        for e in range(1, inner):
            forward(m, 0, (0, 0), (0, e))()

    def arrive(m, k, which=None):
        _, target, valid = steps[k - 1]
        copy = along(m, planes[k], chosen(target, a))
        further = chosen(valid, a)
        hops = [forward(m, k, (0, 0), (f, 0)) for f in range(1, mid)]
        hops += [forward(m, k, (0, 0), (0, e)) for e in range(1, inner)]

        def go():
            copy.wait_recv()
            guard(copy, further)
            for hop in hops:
                hop()

        if which is None:
            go()
        else:
            pl.when(inside == which)(go)

    def come(m, k):
        if k == 1:
            arrive(m, 1)
        else:
            arrive(m, k, 0)
        if k + 1 < outer:
            arrive(m, k + 1, 1)

    def across(m, k, f):
        copies[m, (k, f, 0)].wait_recv()
        for e in range(1, inner):
            forward(m, k, (f, 0), (0, e))()
        if not detour or m != last:
            return
        if k == 0:
            guard(beside(0, chosen([1, 0, 3, 2], a), 1), 1 - inside)
        elif k != 2:
            guard(beside(k, chosen(steps[k - 1][1], a), 3), inside)

    def core(m, k, f, e):
        copies[m, (k, f, e)].wait_recv()

    def source(k, f, e):
        return index_of(dims, planes[k], turned(b, -f, mid), turned(c, -e, inner))

    def drain():
        peer = device(a, 0, 1)
        if group > 1:
            count = outer * (group - 1)
            if not detour:
                sent_all(got.at[:, :count], d_send.at[0], peer)
            for m in range(mats if detour else 0):
                kept = count - 2 if m == last else count
                sent_all(got.at[m, :kept], d_send.at[m], peer)
        if detour:
            sent_all(got.at[0, :2], u_send.at[0], peer)
        if outer > 1:
            @pl.when(inside == 1)
            def _():
                sent_all(got.at[:, :outer + 1], l_send.at[0], peer)

            @pl.when(inside == 0)
            def _():
                sent_all(got.at[:, :1], l_send.at[0], peer)

    return sent_own, come, across, core, source, drain


def reduce_stage(
    dims, n_tensor, groups, rows_ready, entropy, plan,
    dkv, exps, grad_out, mean_out,
    got, rows_v, vec_v, grads, helds, t_send, t_recv,
):
    outer, mid, inner = dims
    n_task = outer * mid * inner
    task, a, b, c = place(dims)
    y = lax.axis_index("tensor")
    tasks, mats, rows, cols = vec_v.shape
    row_blocks, col_blocks = exps.shape[1:3]
    _, come, across, core, source, drain = plan
    fresh = set()

    def take(m, k, f, e):
        own = not (k or f or e)
        if k and not (f or e):
            come(m, k)
        elif f and not e:
            across(m, k, f)
        elif e:
            core(m, k, f, e)
        where = source(k, f, e)
        block = dkv[m] if own else got[m, where]
        term = lax.dot_general(
            rows_v[where], block, (((0,), (0,)), ((), ())), preferred_element_type=F32
        )
        if m in fresh:
            grads[m] += term
        else:
            grads[m] = term
            fresh.add(m)

    high = rows // row_blocks
    wide = cols // col_blocks

    def contracted(m):
        def contract(i, carry):
            these = pl.ds(pl.multiple_of(i * high, 8), high)
            carry = list(carry)
            for j in range(col_blocks):
                across = slice(j * wide, (j + 1) * wide)
                grad = grads[m, these, across]
                for t in range(tasks):
                    term = grad * vec_v[t, m, these, across].astype(F32)
                    term = jnp.sum(term.reshape(high // 8, 8, wide), axis=0)
                    carry[t] = carry[t] + scale_of(exps, t, m, i, j) * term
            return tuple(carry)

        start = tuple(jnp.zeros((8, wide), F32) for _ in range(tasks))
        return lax.fori_loop(0, row_blocks, contract, start)

    rows_ready()
    lines = {}
    turns = [(k, m) for k in range(outer) for m in reversed(range(mats))]
    across_turns = turns[:-mats] + turns[-mats:][::-1]
    for step in range(len(turns) + 2):
        over = step >= len(turns)
        first, then = [], []
        if not over:
            first.append((turns[step], 0, 0))
        if 1 <= step <= len(turns):
            (then if over else first).extend([(across_turns[step - 1], f, 0) for f in range(1, mid)])
            first += [(turns[step - 1], 0, e) for e in range(1, inner)]
        if step >= 2:
            first += [(across_turns[step - 2], f, e) for f in range(1, mid) for e in range(1, inner)]
        for (k, m), f, e in first:
            take(m, k, f, e)
        if step - 2 >= len(turns) - mats:
            m = across_turns[step - 2][1]
            lines[m] = contracted(m)
        for (k, m), f, e in then:
            take(m, k, f, e)
    parts = [
        jnp.sum(lines[m][t], axis=0, keepdims=True) for t in range(tasks) for m in range(mats)
    ]
    entropy = jnp.broadcast_to(entropy / (n_tensor * wide), (1, wide))
    pad = -(len(parts) + 1) % 8
    stack = jnp.concatenate(parts + [entropy, jnp.zeros((pad, wide), F32)], axis=0)
    column = jnp.sum(stack, axis=1, keepdims=True)
    shape = (stack.shape[0], helds[0].shape[2])
    along = lax.broadcasted_iota(jnp.int32, shape, 0) == lax.broadcasted_iota(jnp.int32, shape, 1)
    total = jnp.sum(jnp.where(along, column, 0.0), axis=0, keepdims=True)
    for n, (held, (slot, peers)) in enumerate(zip(helds, groups)):
        held[slot] = total
        for peer in peers:
            send(held.at[slot], held.at[slot], t_send.at[n], t_recv.at[n], peer)
        if peers:
            came_all(held.at[:len(peers)], t_recv.at[n], peers[0])
        total = held[0]
        for k in range(1, len(peers) + 1):
            total = total + held[k]
    tokens = rows_v.shape[1]
    mean_out[...] = total[0:1, tasks * mats:tasks * mats + 1] * (1.0 / (tokens * n_task))
    wide_line = jnp.broadcast_to(total[0:1], (tasks, total.shape[1]))
    spot = lax.broadcasted_iota(jnp.int32, wide_line.shape, 1)
    task_at = lax.broadcasted_iota(jnp.int32, wide_line.shape, 0)
    grid = (mats, total.shape[1])
    mat_at = lax.broadcasted_iota(jnp.int32, grid, 0)
    result = jnp.zeros(grid, F32)
    for m in range(mats):
        column = jnp.sum(jnp.where(spot == mats * task_at + m, wide_line, 0.0), axis=1, keepdims=True)
        row = jnp.sum(jnp.where(spot == task_at, column, 0.0), axis=0, keepdims=True)
        result = jnp.where(mat_at == m, row, result)
    grad_out[...] = result[:, :tasks]
    drain()
    for n, (held, (slot, peers)) in enumerate(zip(helds, groups)):
        if peers:
            sent_all(held.at[:len(peers)], t_send.at[n], peers[0])


def whole_kernel(
    dims, n_tensor, pieces, bunch,
    inputs, queries, vectors, base, exps, coefs,
    att, mean_out, grad_out,
    xin, mg, vec_v, base_v, acc, hold, pout, pin, kv, rows_v, dkv, probs, logs, expos, outs, sums,
    got, grads, q_v, att_v, io_sem, exps_v, coefs_v,
    local_sem, keep_sem, x_send, x_recv, y_send, y_recv, g_send, g_recv, r_send, r_recv, p_send, p_recv,
    s_send, s_recv, d_send, d_recv, l_send, l_recv, u_send, t_send, t_recv, *helds,
):
    n_task = dims[0] * dims[1] * dims[2]
    task = lax.axis_index("task")
    y = lax.axis_index("tensor")
    if len(helds) == 1:
        me, count = task * n_tensor + y, n_task * n_tensor
        others = [turned(me, s, count) for s in range(1, count)]
        groups = [
            (me, [{"task": k // n_tensor, "tensor": lax.rem(k, n_tensor)} for k in others]),
        ]
    else:
        groups = [
            (task, [{"task": turned(task, s, n_task), "tensor": y} for s in range(1, n_task)]),
            (y, [{"task": task, "tensor": turned(y, s, n_tensor)} for s in range(1, n_tensor)]),
        ]

    small = [fetch(exps, exps_v, io_sem.at[2]), fetch(coefs, coefs_v, io_sem.at[3])]
    waiting = []

    def greet():
        meet([peer for _, peers in groups for peer in peers])
        for copy in small:
            copy.wait()

    query_copy = fetch(queries, q_v, io_sem.at[0])
    keys_ready, between, values_ready, rows_ready, drain = project_stage(
        dims, n_tensor, pieces, bunch, inputs, vectors, base, exps_v, coefs_v, greet, kv, rows_v,
        xin, mg, vec_v, base_v, acc, hold, pout, pin,
        local_sem, keep_sem, x_send, x_recv, y_send, y_recv, g_send, g_recv, r_send, r_recv, p_send, p_recv,
    )
    query_copy.wait()
    plan = spread_plan(dims, kv.shape[0], dkv, got, d_send, d_recv, l_send, l_recv, u_send)

    def att_done():
        waiting.append(fetch(att_v, att, io_sem.at[1]))

    exchanged, entropy = attend_stage(
        n_tensor, q_v, kv, att_v, dkv, probs, logs, expos, outs, sums, s_send, s_recv,
        keys_ready, between, values_ready, att_done, plan[0],
    )
    reduce_stage(
        dims, n_tensor, groups, rows_ready, entropy, plan,
        dkv, exps_v, grad_out, mean_out,
        got, rows_v, vec_v, grads, helds, t_send, t_recv,
    )
    drain()
    for copy in exchanged:
        copy.wait_send()
    for copy in waiting:
        copy.wait()


def local(inputs, queries, task_vectors, base_weights, scale_exps, coefs):
    n_task = lax.axis_size("task")
    n_tensor = lax.axis_size("tensor")
    dims = factors(n_task)
    outer, mid, inner = dims
    group = mid * inner
    tokens = inputs.shape[0]
    tasks, mats, rows, cols = task_vectors.shape
    heads = cols // HEAD
    pieces = math.gcd(tokens // 16, 6)
    bunch = math.gcd(pieces, 2)
    hbm = pl.BlockSpec(memory_space=pltpu.HBM)
    anywhere = pl.BlockSpec(memory_space=pl.ANY)
    vmem = pl.BlockSpec(memory_space=pltpu.VMEM)
    dma = pltpu.SemaphoreType.DMA
    slots = [n_task * n_tensor] if n_task * n_tensor <= 64 else [n_task, n_tensor]

    def pair(count):
        return [dma((count,)), dma((count,))]

    attended, mean_entropy, coef_grad = pl.pallas_call(
        functools.partial(whole_kernel, dims, n_tensor, pieces, bunch),
        out_shape=(
            jax.ShapeDtypeStruct(queries.shape, BF16),
            jax.ShapeDtypeStruct((1, 1), F32),
            jax.ShapeDtypeStruct((mats, tasks), F32),
        ),
        in_specs=[hbm] * 6,
        out_specs=(anywhere, vmem, vmem),
        scratch_shapes=[
            pltpu.VMEM((outer, tokens, group * rows), BF16),
            pltpu.VMEM((group, mats, rows, cols), BF16),
            pltpu.VMEM(task_vectors.shape, BF16),
            pltpu.VMEM(base_weights.shape, BF16),
            pltpu.VMEM((mats, tokens, cols), F32),
            pltpu.VMEM((mats, tokens, cols), F32),
            pltpu.VMEM((outer, mats, tokens, cols), BF16),
            pltpu.VMEM((outer, mats, tokens, cols), BF16),
            pltpu.VMEM((mats, tokens, cols), BF16),
            pltpu.VMEM((n_task, tokens, rows), BF16),
            pltpu.VMEM((mats, tokens, cols), BF16),
            pltpu.VMEM((heads, tokens, GROUP * tokens), F32),
            pltpu.VMEM((heads, GROUP * tokens, HEAD), F32),
            pltpu.VMEM((heads, GROUP * tokens, HEAD), F32),
            pltpu.VMEM((heads, GROUP * tokens, HEAD), BF16),
            pltpu.VMEM((n_tensor, 8, tokens), F32),
            pltpu.VMEM((mats, n_task, tokens, cols), BF16),
            pltpu.VMEM((mats, rows, cols), F32),
            pltpu.VMEM(queries.shape, BF16),
            pltpu.VMEM(queries.shape, BF16),
            dma((4,)),
            pltpu.SMEM((mats, *scale_exps.shape[2:], tasks), jnp.int32), pltpu.SMEM((mats, tasks), F32),
            dma((2 + mats,)), dma((1,)),
            dma((1,)), dma((outer * pieces,)),
            dma((1,)), dma((pieces,)),
            dma((1,)), dma((mats * group,)),
            dma((1,)), dma((1,)),
            dma((1,)), dma((mats * (pieces + 2),)),
            *pair(n_tensor),
            dma((mats,)), dma((mats * n_task,)),
            dma((1,)), dma((mats * outer,)),
            dma((1,)),
            *pair(len(slots)),
            *[pltpu.VMEM((count, 1, 128), F32) for count in slots],
        ],
        compiler_params=pltpu.CompilerParams(
            collective_id=0, has_side_effects=True, vmem_limit_bytes=VMEM_BYTES
        ),
        name="whole",
    )(
        *[
            pltpu.with_memory_space_constraint(value, pltpu.HBM)
            for value in (
                inputs, queries, task_vectors, base_weights, scale_exps.transpose(1, 2, 3, 0), coefs.T
            )
        ]
    )
    return (attended, mean_entropy[0, 0], coef_grad.T)


def solution(mesh):
    return jax.shard_map(
        local,
        mesh=mesh,
        in_specs=(
            P("task", None),
            P("task", "tensor"),
            P(None, None, "task", "tensor"),
            P(None, "task", "tensor"),
            P(None, None, "task", "tensor"),
            P(),
        ),
        out_specs=(P("task", "tensor"), P(), P()),
        check_vma=False,
    )
```
